512 devices in a mesh: tok: 64 (over y_lo, z, core), row: 8 (over y_hi, x).
Axes of the slice: x: 4, y: 4 (y_hi: 2, y_lo: 2; y = y_hi * 2 + y_lo), z: 16, core: 2. Of those that a mesh axis runs over, the one named last changes fastest.
Arguments:
- calib: bfloat16 [8192, 4096], P('row', 'tok'), may hold values from -8 to 8
- base_weight: bfloat16 [8192, 4096], P('tok', 'row'), may hold values from -6 to 6
- keep_blocks: int32 [64, 16], replicated, may hold values from 0 to 31, all different within a row
Outputs:
- refined: bfloat16 [8192, 4096], P('tok', 'row')
The draws below stay inside these ranges and needn't reach their ends.
Inputs may be any that keep to these rules, and one draw needn't show every extreme that they name: `keep_blocks`: each row lists 16 different block columns, and every block column is listed in some row.
All inputs are finite; a program needn't handle non-finite values.
Results may differ from the reference program's by a relative error of at most 0.0085.
Values may be sent and summed in bfloat16 or wider, within the bound.
No kernel may reach another device: no remote copies, remote signals or barrier semaphores. Data moves between devices by JAX's collectives and lax.ppermute only.
A program may use at most 64 MiB of HBM per device.

```python
import math
import jax
import jax.numpy as jnp
from jax import lax

D = 4096
OUT = 8192
BLOCK = 128
KEEP = 16
ITERS = 2
TOKENS = 8192


def draw_calib(key, part):
    variance = 6.4 / (1.0 + math.sqrt(D / (2.0 * TOKENS))) ** 2
    extent = (TOKENS, D)
    drawn = jnp.clip(math.sqrt(variance) * jax.random.normal(key, extent, jnp.float32), -8.0, 8.0)
    return drawn.astype(jnp.bfloat16)


def block_levels(stream_key, dims, pieces, smallest, top_value):
    gain = 1.0
    for axis_at, blocks in pieces:
        draws = jax.random.uniform(jax.random.fold_in(jax.random.fold_in(stream_key, 6), axis_at), (blocks,), jnp.float32, smallest / len(pieces), top_value / len(pieces))
        gain = gain * jnp.repeat(jnp.exp(draws), dims[axis_at] // blocks).reshape((-1,) + (1,) * (len(dims) - 1 - axis_at))
    return gain


def picks_of(key, rows, count, top, lift):
    ranking = jax.random.permutation(jax.random.fold_in(key, 1), count)
    pull = ranking
    for power in range(3):
        pull = pull * pull // count
    pull = pull * lift // count
    tickets = jax.random.randint(jax.random.fold_in(key, 2), (rows, count), 0, 4096) + pull
    holders = jax.random.permutation(jax.random.fold_in(key, 3), rows)[jnp.arange(count) % rows]
    tickets = jnp.where(jnp.arange(rows)[:, None] == holders[None, :], 1 << 14, tickets)
    score = tickets * count + jnp.arange(count)
    return lax.top_k(score.astype(jnp.int32), top)[1].astype(jnp.int32)


def gaussian(stream_key, shape, width, bound, shards=(), kind=jnp.bfloat16):
    entries = width * jax.random.normal(stream_key, shape, jnp.float32)
    if shards:
        entries = entries * block_levels(stream_key, shape, shards, -0.22, 0.18)
    return jnp.clip(entries, -bound, bound).astype(kind)


def setup_inputs(seed: int = 0) -> dict:
    key_of = jax.random.split(jax.random.key(seed), 4)
    return {
        "calib": draw_calib(jax.random.fold_in(key_of[3], 71), 0),
        "base_weight": gaussian(key_of[1], (OUT, D), 1.0, 6.0, ((0, 64), (1, 8))),
        "keep_blocks": picks_of(key_of[2], (OUT // BLOCK), D // BLOCK, KEEP, 4096),
    }


def expand_keep(keep_blocks, ncols):
    labels = jnp.arange(ncols, dtype=jnp.int32)
    hits = (keep_blocks[:, :, None] == labels[None, None, :]).astype(jnp.float32)
    block_map = jnp.sum(hits, axis=1)
    return jnp.repeat(jnp.repeat(block_map, BLOCK, axis=0), BLOCK, axis=1)


def reference(calib, base_weight, keep_blocks):
    gram = (jnp.dot(calib.T, calib, preferred_element_type=jnp.float32) / TOKENS).astype(jnp.bfloat16)
    keep = expand_keep(keep_blocks, D // BLOCK)
    base_float = base_weight.astype(jnp.float32)
    weight = (keep * base_float).astype(jnp.bfloat16)
    for step in range(ITERS):
        diff = (weight.astype(jnp.float32) - base_float).astype(jnp.bfloat16)
        grad = jnp.dot(diff, gram, preferred_element_type=jnp.float32)
        weight = (weight.astype(jnp.float32) - 0.25 * keep * grad).astype(jnp.bfloat16)
    return weight
```

```python
import functools

import jax
import jax.numpy as jnp
from jax import lax
from jax.experimental import pallas as pl
from jax.experimental.pallas import tpu as pltpu
from jax.sharding import Mesh, PartitionSpec as P

BLOCK = 128
RATE = 0.25
NT = (((1,), (1,)), ((), ()))
AXES = ("ylo", "zh", "zl", "core", "yhi", "x")
SIZES = (2, 4, 4, 2, 2, 4)
TOK = ("ylo", "zh", "zl", "core")
ROW = ("yhi", "x")
SWAP = ((0, 1), (1, 0))


def vmem():
    return pl.BlockSpec(memory_space=pltpu.VMEM)


def smem():
    return pl.BlockSpec(memory_space=pltpu.SMEM)


def partial_gram_kernel(where, rows, own, other, out):
    ylo = where[0]
    half = out.shape[3]
    for j, cols in enumerate((own, other)):
        term = lax.dot_general(cols[...], rows[...], NT, preferred_element_type=jnp.float32)
        term = term.astype(jnp.bfloat16)
        first = (ylo ^ j) * 4
        for c in range(2):
            piece = term[:, c * half : (c + 1) * half]
            out[c, pl.ds(first, 4)] = piece.reshape(4, BLOCK, half)


def partial_gram(where, rows, own, other):
    k = rows.shape[0]
    return pl.pallas_call(
        partial_gram_kernel,
        out_shape=jax.ShapeDtypeStruct((2, 8, BLOCK, k // 2), jnp.bfloat16),
        in_specs=[smem(), vmem(), vmem(), vmem()],
        out_specs=vmem(),
        name="partial_gram",
        cost_estimate=pl.CostEstimate(
            flops=4 * k * k * rows.shape[1], bytes_accessed=5 * rows.size, transcendentals=0
        ),
    )(where, rows, own, other)


def step_kernel(last, where, flags, diffs, g00, g10, g01, g11, weight, base, *outs):
    ylo, core = where[0], where[1]
    half = g00.shape[2]
    total = jnp.zeros(weight.shape, jnp.float32)
    for dy, dc, gram in ((0, 0, g00), (0, 1, g01), (1, 0, g10), (1, 1, g11)):
        lanes = pl.ds(pl.multiple_of((core ^ dc) * half, half), half)
        for h in range(4):
            total += lax.dot_general(
                diffs[(ylo ^ dy) * 4 + h, :, lanes], gram[h], NT,
                preferred_element_type=jnp.float32,
            )
    block = lax.broadcasted_iota(jnp.int32, weight.shape, 1) // BLOCK
    keep = jnp.zeros(weight.shape, jnp.float32)
    for b in range(weight.shape[1] // BLOCK):
        keep = jnp.where(block == b, flags[b].astype(jnp.float32), keep)
    new = (weight[...].astype(jnp.float32) - RATE * keep * total).astype(jnp.bfloat16)
    outs[0][...] = new
    if not last:
        diff = (new.astype(jnp.float32) - base[...].astype(jnp.float32)).astype(jnp.bfloat16)
        for i in range(outs[1].shape[0]):
            outs[1][i] = diff


def step(last, where, flags, diffs, grams, weight, base):
    shape = jax.ShapeDtypeStruct(weight.shape, weight.dtype)
    outs = (shape,) if last else (shape, jax.ShapeDtypeStruct(diffs.shape, diffs.dtype))
    return pl.pallas_call(
        functools.partial(step_kernel, last),
        out_shape=outs,
        in_specs=[smem(), smem()] + [vmem()] * 7,
        out_specs=tuple(vmem() for _ in outs),
        name="last_step" if last else "first_step",
        compiler_params=pltpu.CompilerParams(vmem_limit_bytes=32 << 20),
        cost_estimate=pl.CostEstimate(
            flops=2 * diffs.size * weight.shape[1], bytes_accessed=12 * diffs.size // 2,
            transcendentals=0,
        ),
    )(where, flags, diffs, *grams, weight, base)


def spread(x, axes, n):
    return lax.all_to_all(jnp.broadcast_to(x[None], (n,) + x.shape), axes, 0, 0, tiled=True)


def on_device(calib, base_weight, keep_blocks):
    ylo, core = lax.axis_index("ylo"), lax.axis_index("core")
    tok_pos, row_pos = lax.axis_index(TOK), lax.axis_index(ROW)
    rows, cols = base_weight.shape
    tokens = calib.shape[0] * 8
    where = jnp.stack([ylo, core]).astype(jnp.int32)
    kept = lax.dynamic_slice(keep_blocks, (tok_pos, 0), (1, keep_blocks.shape[1]))
    nblocks = cols // BLOCK
    mine = row_pos * nblocks + jnp.arange(nblocks, dtype=jnp.int32)
    flags = jnp.any(kept[0][:, None] == mine[None, :], axis=0).astype(jnp.int32)
    keep = jnp.repeat(flags.astype(jnp.float32), BLOCK)[None, :]
    base_float = base_weight.astype(jnp.float32)
    weight = (keep * base_float).astype(jnp.bfloat16)
    diff = (weight.astype(jnp.float32) - base_float).astype(jnp.bfloat16)
    diff, calib = lax.optimization_barrier((diff, calib))
    diffs = lax.all_gather(diff, ROW, axis=0)

    feats = lax.all_to_all(calib.T, "core", 1, 0, tiled=True)
    own = lax.all_gather(feats, "zh", axis=0, tiled=True)
    other = lax.ppermute(own, "ylo", SWAP)
    mates = lax.all_gather(feats, "zl", axis=0, tiled=True)
    term = partial_gram(where, mates, own, other)
    half = term.shape[3]
    terms = lax.all_to_all(term.reshape(16, BLOCK, half), ("core",) + ROW, 0, 0, tiled=True)
    gram = (jnp.sum(terms.astype(jnp.float32), axis=0) / tokens).astype(jnp.bfloat16)

    g00 = spread(gram, ("zh", "zl"), 16).reshape(4, 4 * BLOCK, half)
    g10 = lax.ppermute(g00, "ylo", SWAP)
    g01 = lax.ppermute(g00, "core", SWAP)
    g11 = lax.ppermute(g10, "core", SWAP)
    grams = (g00, g10, g01, g11)

    weight, sent = step(False, where, flags, diffs, grams, weight, base_weight)
    diffs = lax.all_to_all(sent, ROW, 0, 0, tiled=True)
    return step(True, where, flags, diffs, grams, weight, base_weight)[0]


def solution(mesh):
    split = Mesh(mesh.devices.reshape(SIZES), AXES)
    return jax.shard_map(
        on_device,
        mesh=split,
        in_specs=(P(ROW, TOK), P(TOK, ROW), P()),
        out_specs=P(TOK, ROW),
        check_vma=False,
    )
```

```python
import functools

import jax
import jax.numpy as jnp
from jax import lax
from jax.experimental import pallas as pl
from jax.experimental.pallas import tpu as pltpu
from jax.sharding import Mesh, PartitionSpec as P

BLOCK = 128
RATE = 0.25
NT = (((1,), (1,)), ((), ()))
AXES = ("ylo", "zh", "zl", "core", "yhi", "x")
SIZES = (2, 4, 4, 2, 2, 4)
TOK = ("ylo", "zh", "zl", "core")
ROW = ("yhi", "x")
SWAP = ((0, 1), (1, 0))
CLASSES = (0, 1, 3, 2)


def from_z(*steps):
    return [((z + s) % 16 * 2 + c, z * 2 + c) for z in range(16) for c, s in enumerate(steps)]


def vmem():
    return pl.BlockSpec(memory_space=pltpu.VMEM)


def smem():
    return pl.BlockSpec(memory_space=pltpu.SMEM)


def partial_gram_kernel(where, rows, own, other, out):
    ylo = where[0]
    half = out.shape[3]
    for j, cols in enumerate((own, other)):
        term = lax.dot_general(cols[...], rows[...], NT, preferred_element_type=jnp.float32)
        term = term.astype(jnp.bfloat16)
        first = (ylo ^ j) * 4
        for c in range(2):
            piece = term[:, c * half : (c + 1) * half]
            out[c, pl.ds(first, 4)] = piece.reshape(4, BLOCK, half)


def partial_gram(where, rows, own, other):
    k = rows.shape[0]
    return pl.pallas_call(
        partial_gram_kernel,
        out_shape=jax.ShapeDtypeStruct((2, 8, BLOCK, k // 2), jnp.bfloat16),
        in_specs=[smem(), vmem(), vmem(), vmem()],
        out_specs=vmem(),
        name="partial_gram",
        cost_estimate=pl.CostEstimate(
            flops=4 * k * k * rows.shape[1], bytes_accessed=5 * rows.size, transcendentals=0
        ),
    )(where, rows, own, other)


def step_kernel(last, where, flags, diffs, *refs):
    grams, (weight, base), outs, total = refs[:16], refs[16:18], refs[18:-1], refs[-1]
    ylo, zl, core = where[0], where[1], where[2]
    half = grams[0].shape[2]
    for j, shift in enumerate(CLASSES):
        part = jnp.zeros((weight.shape[0], BLOCK), jnp.float32)
        for dy in range(2):
            for dc in range(2):
                gram = grams[(dy * 2 + dc) * 4 + j]
                lanes = pl.ds(pl.multiple_of((core ^ dc) * half, half), half)
                for h in range(4):
                    part += lax.dot_general(
                        diffs[(ylo ^ dy) * 4 + h, :, lanes], gram[h], NT,
                        preferred_element_type=jnp.float32,
                    )
        place = lax.rem(zl + shift, 4) * BLOCK
        total[:, pl.ds(pl.multiple_of(place, BLOCK), BLOCK)] = part
    block = lax.broadcasted_iota(jnp.int32, weight.shape, 1) // BLOCK
    keep = jnp.zeros(weight.shape, jnp.float32)
    for b in range(weight.shape[1] // BLOCK):
        keep = jnp.where(block == b, flags[b].astype(jnp.float32), keep)
    new = (weight[...].astype(jnp.float32) - RATE * keep * total[...]).astype(jnp.bfloat16)
    outs[0][...] = new
    if not last:
        diff = (new.astype(jnp.float32) - base[...].astype(jnp.float32)).astype(jnp.bfloat16)
        for i in range(outs[1].shape[0]):
            outs[1][i] = diff


def step(last, where, flags, diffs, grams, weight, base):
    shape = jax.ShapeDtypeStruct(weight.shape, weight.dtype)
    outs = (shape,) if last else (shape, jax.ShapeDtypeStruct(diffs.shape, diffs.dtype))
    return pl.pallas_call(
        functools.partial(step_kernel, last),
        out_shape=outs,
        in_specs=[smem(), smem()] + [vmem()] * (len(grams) + 3),
        out_specs=tuple(vmem() for _ in outs),
        scratch_shapes=[pltpu.VMEM(weight.shape, jnp.float32)],
        name="last_step" if last else "first_step",
        compiler_params=pltpu.CompilerParams(vmem_limit_bytes=32 << 20),
        cost_estimate=pl.CostEstimate(
            flops=2 * diffs.size * weight.shape[1], bytes_accessed=12 * diffs.size // 2,
            transcendentals=0,
        ),
    )(where, flags, diffs, *grams, weight, base)


def on_device(calib, base_weight, keep_blocks):
    tok_pos, row_pos = lax.axis_index(TOK), lax.axis_index(ROW)
    rows, cols = base_weight.shape
    tokens = calib.shape[0] * 8
    where = jnp.stack([lax.axis_index(a) for a in ("ylo", "zl", "core")]).astype(jnp.int32)
    kept = lax.dynamic_slice(keep_blocks, (tok_pos, 0), (1, keep_blocks.shape[1]))
    nblocks = cols // BLOCK
    labels = row_pos * nblocks + jnp.arange(nblocks, dtype=jnp.int32)
    flags = jnp.any(kept[0][:, None] == labels[None, :], axis=0).astype(jnp.int32)
    keep = jnp.repeat(flags.astype(jnp.float32), BLOCK)[None, :]
    base_float = base_weight.astype(jnp.float32)
    weight = (keep * base_float).astype(jnp.bfloat16)
    diff = (weight.astype(jnp.float32) - base_float).astype(jnp.bfloat16)
    diff, calib = lax.optimization_barrier((diff, calib))
    diffs = lax.all_gather(diff, ROW, axis=0)

    feats = lax.all_to_all(calib.T, "core", 1, 0, tiled=True)
    own = lax.all_gather(feats, "zh", axis=0, tiled=True)
    other = lax.ppermute(own, "ylo", SWAP)
    mates = lax.all_gather(feats, "zl", axis=0, tiled=True)
    term = partial_gram(where, mates, own, other)
    half = term.shape[3]
    diffs, term = lax.optimization_barrier((diffs, term))
    terms = lax.all_to_all(term.reshape(16, BLOCK, half), ("core",) + ROW, 0, 0, tiled=True)
    gram = (jnp.sum(terms.astype(jnp.float32), axis=0) / tokens).astype(jnp.bfloat16)

    line = ("zh", "zl", "core")
    mine = lax.all_gather(gram, "zh", axis=0)
    near = [mine] + [lax.ppermute(mine, line, from_z(*s)) for s in ((1, 1), (-1, -1), (2, -2))]
    far = [lax.ppermute(g, "ylo", SWAP) for g in near]
    near_mate = [lax.ppermute(g, "core", SWAP) for g in near]
    far_mate = [lax.ppermute(g, "core", SWAP) for g in far]
    grams = near + near_mate + far + far_mate

    weight, sent = step(False, where, flags, diffs, grams, weight, base_weight)
    diffs = lax.all_to_all(sent, ROW, 0, 0, tiled=True)
    return step(True, where, flags, diffs, grams, weight, base_weight)[0]


def solution(mesh):
    split = Mesh(mesh.devices.reshape(SIZES), AXES)
    return jax.shard_map(
        on_device,
        mesh=split,
        in_specs=(P(ROW, TOK), P(TOK, ROW), P()),
        out_specs=P(TOK, ROW),
        check_vma=False,
    )
```

```python
import functools

import jax
import jax.numpy as jnp
from jax import lax
from jax.experimental import pallas as pl
from jax.experimental.pallas import tpu as pltpu
from jax.sharding import Mesh, PartitionSpec as P

BLOCK = 128
RATE = 0.25
NT = (((1,), (1,)), ((), ()))
AXES = ("ylo", "zh", "zl", "core", "yhi", "x")
SIZES = (2, 4, 4, 2, 2, 4)
TOK = ("ylo", "zh", "zl", "core")
ROW = ("yhi", "x")
SWAP = ((0, 1), (1, 0))
CLASSES = (0, 1, 3, 2)


def from_z(*steps):
    return [((z + s) % 16 * 2 + c, z * 2 + c) for z in range(16) for c, s in enumerate(steps)]


def vmem():
    return pl.BlockSpec(memory_space=pltpu.VMEM)


def smem():
    return pl.BlockSpec(memory_space=pltpu.SMEM)


def partial_gram_kernel(where, rows, own, other, out):
    ylo = where[0]
    half = out.shape[3]
    for j, cols in enumerate((own, other)):
        term = lax.dot_general(cols[...], rows[...], NT, preferred_element_type=jnp.float32)
        term = term.astype(jnp.bfloat16)
        first = (ylo ^ j) * 4
        for c in range(2):
            piece = term[:, c * half : (c + 1) * half]
            out[c, pl.ds(first, 4)] = piece.reshape(4, BLOCK, half)


def partial_gram(where, rows, own, other):
    k = rows.shape[0]
    return pl.pallas_call(
        partial_gram_kernel,
        out_shape=jax.ShapeDtypeStruct((2, 8, BLOCK, k // 2), jnp.bfloat16),
        in_specs=[smem(), vmem(), vmem(), vmem()],
        out_specs=vmem(),
        name="partial_gram",
        compiler_params=pltpu.CompilerParams(vmem_limit_bytes=8 << 20),
        cost_estimate=pl.CostEstimate(
            flops=4 * k * k * rows.shape[1], bytes_accessed=5 * rows.size, transcendentals=0
        ),
    )(where, rows, own, other)


def step_kernel(last, where, flags, diffs, *refs):
    near, near_mate, far, far_mate = refs[:4], refs[4], refs[5:9], refs[9:13]
    grams = (*near, *(near_mate.at[j] for j in range(4)), *far, *far_mate)
    (weight, base), outs, total = refs[13:15], refs[15:-1], refs[-1]
    ylo, zl, core = where[0], where[1], where[2]
    half = grams[0].shape[2]
    for j, shift in enumerate(CLASSES):
        part = jnp.zeros((weight.shape[0], BLOCK), jnp.float32)
        for dy in range(2):
            for dc in range(2):
                gram = grams[(dy * 2 + dc) * 4 + j]
                lanes = pl.ds(pl.multiple_of((core ^ dc) * half, half), half)
                for h in range(4):
                    part += lax.dot_general(
                        diffs[(ylo ^ dy) * 4 + h, :, lanes], gram[h], NT,
                        preferred_element_type=jnp.float32,
                    )
        place = lax.rem(zl + shift, 4) * BLOCK
        total[:, pl.ds(pl.multiple_of(place, BLOCK), BLOCK)] = part
    block = lax.broadcasted_iota(jnp.int32, weight.shape, 1) // BLOCK
    keep = jnp.zeros(weight.shape, jnp.float32)
    for b in range(weight.shape[1] // BLOCK):
        keep = jnp.where(block == b, flags[b].astype(jnp.float32), keep)
    new = (weight[...].astype(jnp.float32) - RATE * keep * total[...]).astype(jnp.bfloat16)
    outs[0][...] = new
    if not last:
        diff = (new.astype(jnp.float32) - base[...].astype(jnp.float32)).astype(jnp.bfloat16)
        for i in range(outs[1].shape[0]):
            outs[1][i] = diff


def step(last, where, flags, diffs, grams, weight, base):
    shape = jax.ShapeDtypeStruct(weight.shape, weight.dtype)
    outs = (shape,) if last else (shape, jax.ShapeDtypeStruct(diffs.shape, diffs.dtype))
    return pl.pallas_call(
        functools.partial(step_kernel, last),
        out_shape=outs,
        in_specs=[smem(), smem()] + [vmem()] * (len(grams) + 3),
        out_specs=tuple(vmem() for _ in outs),
        scratch_shapes=[pltpu.VMEM(weight.shape, jnp.float32)],
        name="last_step" if last else "first_step",
        compiler_params=pltpu.CompilerParams(vmem_limit_bytes=16 << 20),
        cost_estimate=pl.CostEstimate(
            flops=2 * diffs.size * weight.shape[1], bytes_accessed=12 * diffs.size // 2,
            transcendentals=0,
        ),
    )(where, flags, diffs, *grams, weight, base)


def pack_kernel(*refs):
    for i, ref in enumerate(refs[:-1]):
        refs[-1][i] = ref[...]


def pack(parts):
    part = parts[0]
    return pl.pallas_call(
        pack_kernel,
        out_shape=jax.ShapeDtypeStruct((len(parts),) + part.shape, part.dtype),
        in_specs=[vmem()] * len(parts),
        out_specs=vmem(),
        name="pack",
        compiler_params=pltpu.CompilerParams(vmem_limit_bytes=4 << 20),
        cost_estimate=pl.CostEstimate(
            flops=0, bytes_accessed=4 * len(parts) * part.size, transcendentals=0
        ),
    )(*parts)


def on_device(calib, base_weight, keep_blocks):
    tok_pos, row_pos = lax.axis_index(TOK), lax.axis_index(ROW)
    rows, cols = base_weight.shape
    tokens = calib.shape[0] * 8
    where = jnp.stack([lax.axis_index(a) for a in ("ylo", "zl", "core")]).astype(jnp.int32)
    kept = lax.dynamic_slice(keep_blocks, (tok_pos, 0), (1, keep_blocks.shape[1]))
    nblocks = cols // BLOCK
    labels = row_pos * nblocks + jnp.arange(nblocks, dtype=jnp.int32)
    flags = jnp.any(kept[0][:, None] == labels[None, :], axis=0).astype(jnp.int32)
    keep = jnp.repeat(flags.astype(jnp.float32), BLOCK)[None, :]
    base_float = base_weight.astype(jnp.float32)
    weight = (keep * base_float).astype(jnp.bfloat16)
    diff = (weight.astype(jnp.float32) - base_float).astype(jnp.bfloat16)
    diff, calib = lax.optimization_barrier((diff, calib))
    diffs = lax.all_gather(diff, ROW, axis=0)

    feats = lax.all_to_all(calib.T, "core", 1, 0, tiled=True)
    own = lax.all_gather(feats, "zh", axis=0, tiled=True)
    other = lax.ppermute(own, "ylo", SWAP)
    mates = lax.all_gather(feats, "zl", axis=0, tiled=True)
    term = partial_gram(where, mates, own, other)
    half = term.shape[3]
    terms = lax.all_to_all(term.reshape(16, BLOCK, half), ("core",) + ROW, 0, 0, tiled=True)
    diffs, terms = lax.optimization_barrier((diffs, terms))
    gram = (jnp.sum(terms.astype(jnp.float32), axis=0) / tokens).astype(jnp.bfloat16)

    line = ("zh", "zl", "core")
    mine = lax.all_to_all(jnp.broadcast_to(gram[None], (4,) + gram.shape), "zh", 0, 0, tiled=True)
    up, down, two = from_z(1, 1), from_z(-1, -1), from_z(2, -2)
    far = lax.ppermute(mine, "ylo", SWAP)
    near = [mine] + [lax.ppermute(mine, line, s) for s in (up, down, two)]
    far = [far] + [lax.ppermute(g, "ylo", SWAP) for g in near[1:3]] + [lax.ppermute(far, line, two)]
    far_mate = [lax.ppermute(g, "core", SWAP) for g in far]
    ahead = [far[2], far_mate[0], far_mate[1], far_mate[3]]
    far[2], far_mate[0], far_mate[1], far_mate[3], *held = lax.optimization_barrier((*ahead, *near))
    near_mate = lax.ppermute(pack(held), "core", SWAP)
    grams = near + [near_mate] + far + far_mate

    weight, sent = step(False, where, flags, diffs, grams, weight, base_weight)
    diffs = lax.all_to_all(sent, ROW, 0, 0, tiled=True)
    return step(True, where, flags, diffs, grams, weight, base_weight)[0]


def solution(mesh):
    split = Mesh(mesh.devices.reshape(SIZES), AXES)
    return jax.shard_map(
        on_device,
        mesh=split,
        in_specs=(P(ROW, TOK), P(TOK, ROW), P()),
        out_specs=P(TOK, ROW),
        check_vma=False,
    )
```

```python
import functools

import jax
import jax.numpy as jnp
from jax import lax
from jax.experimental import pallas as pl
from jax.experimental.pallas import tpu as pltpu
from jax.sharding import Mesh, PartitionSpec as P

BLOCK = 128
RATE = 0.25
NT = (((1,), (1,)), ((), ()))
AXES = ("ylo", "zh", "zl", "core", "yhi", "x")
SIZES = (2, 4, 4, 2, 2, 4)
TOK = ("ylo", "zh", "zl", "core")
ROW = ("yhi", "x")
SWAP = ((0, 1), (1, 0))
CLASSES = (0, 1, 3, 2)


def from_z(*steps):
    return [((z + s) % 16 * 2 + c, z * 2 + c) for z in range(16) for c, s in enumerate(steps)]


def vmem():
    return pl.BlockSpec(memory_space=pltpu.VMEM)


def smem():
    return pl.BlockSpec(memory_space=pltpu.SMEM)


def by_core(x):
    chunk = BLOCK // 2
    order = [2 * i + c for c in range(2) for i in range(x.shape[1] // BLOCK)]
    return jnp.concatenate([x[:, i * chunk : (i + 1) * chunk] for i in order], axis=1)


def start_kernel(kept, base, weight, diff, keep_out):
    tok = lax.axis_index(TOK)
    first = lax.axis_index(ROW) * (base.shape[1] // BLOCK)
    block = lax.broadcasted_iota(jnp.int32, base.shape, 1) // BLOCK
    keep = jnp.zeros(base.shape, jnp.float32)
    for b in range(base.shape[1] // BLOCK):
        listed = jnp.int32(0)
        for j in range(kept.shape[0]):
            listed = jnp.where(kept[j, tok] == first + b, 1, listed)
        keep = jnp.where(block == b, listed.astype(jnp.float32), keep)
    base_float = base[...].astype(jnp.float32)
    new = (keep * base_float).astype(jnp.bfloat16)
    weight[...] = new
    keep_out[...] = keep
    diff[...] = by_core((new.astype(jnp.float32) - base_float).astype(jnp.bfloat16))


def start(keep_blocks, base):
    bf16 = jax.ShapeDtypeStruct(base.shape, base.dtype)
    return pl.pallas_call(
        start_kernel,
        out_shape=(bf16, bf16, jax.ShapeDtypeStruct(base.shape, jnp.float32)),
        in_specs=[smem(), vmem()],
        out_specs=(vmem(),) * 3,
        name="start",
        compiler_params=pltpu.CompilerParams(vmem_limit_bytes=4 << 20),
    )(keep_blocks.T, base)


def partial_gram_kernel(rows, s00, s10, s01, s11, out):
    ylo, core = lax.axis_index("ylo"), lax.axis_index("core")
    chunk = BLOCK // 2
    for dy, dc, cols in ((0, 0, s00), (1, 0, s10), (0, 1, s01), (1, 1, s11)):
        term = lax.dot_general(cols[...], rows[...], NT, preferred_element_type=jnp.float32)
        term = term.astype(jnp.bfloat16).reshape(4, chunk, rows.shape[0])
        half = pl.ds(pl.multiple_of((core ^ dc) * chunk, chunk), chunk)
        out[pl.ds((ylo ^ dy) * 4, 4), half, :] = term


def partial_gram(rows, *cols):
    k = rows.shape[0]
    return pl.pallas_call(
        partial_gram_kernel,
        out_shape=jax.ShapeDtypeStruct((8, BLOCK, k), jnp.bfloat16),
        in_specs=[vmem()] * 5,
        out_specs=vmem(),
        name="partial_gram",
        compiler_params=pltpu.CompilerParams(vmem_limit_bytes=8 << 20),
        cost_estimate=pl.CostEstimate(
            flops=8 * k * k * rows.shape[1], bytes_accessed=12 * rows.size, transcendentals=0
        ),
    )(rows, *cols)


def step_kernel(last, diffs, *refs):
    near, near_mate, far, far_mate = refs[:4], refs[4], refs[5:9], refs[9]
    (weight, base, keep), outs, total = refs[10:13], refs[13:-1], refs[-1]
    ylo, zl, core = (lax.axis_index(a) for a in ("ylo", "zl", "core"))
    half = near[0].shape[2]
    for j, shift in enumerate(CLASSES):
        part = jnp.zeros((weight.shape[0], BLOCK), jnp.float32)
        for dy, dc, gram in (
            (0, 0, near[j]), (0, 1, near_mate.at[j]), (1, 0, far[j]), (1, 1, far_mate.at[j])
        ):
            lanes = pl.ds(pl.multiple_of((core ^ dc) * half, half), half)
            for h in range(4):
                part += lax.dot_general(
                    diffs[(ylo ^ dy) * 4 + h, :, lanes], gram[h], NT,
                    preferred_element_type=jnp.float32,
                )
        place = lax.rem(zl + shift, 4) * BLOCK
        total[:, pl.ds(pl.multiple_of(place, BLOCK), BLOCK)] = part
    old = weight[...].astype(jnp.float32)
    new = (old - RATE * keep[...] * total[...]).astype(jnp.bfloat16)
    outs[0][...] = new
    if not last:
        diff = (new.astype(jnp.float32) - base[...].astype(jnp.float32)).astype(jnp.bfloat16)
        diff = by_core(diff)
        for i in range(outs[1].shape[0]):
            outs[1][i] = diff


def step(last, diffs, grams, weight, base, keep):
    shape = jax.ShapeDtypeStruct(weight.shape, weight.dtype)
    outs = (shape,) if last else (shape, jax.ShapeDtypeStruct(diffs.shape, diffs.dtype))
    return pl.pallas_call(
        functools.partial(step_kernel, last),
        out_shape=outs,
        in_specs=[vmem()] * (len(grams) + 4),
        out_specs=tuple(vmem() for _ in outs),
        scratch_shapes=[pltpu.VMEM(weight.shape, jnp.float32)],
        name="last_step" if last else "first_step",
        compiler_params=pltpu.CompilerParams(vmem_limit_bytes=16 << 20),
        cost_estimate=pl.CostEstimate(
            flops=2 * diffs.size * weight.shape[1], bytes_accessed=12 * diffs.size // 2,
            transcendentals=0,
        ),
    )(diffs, *grams, weight, base, keep)


def pack_kernel(*refs):
    for i, ref in enumerate(refs[:-1]):
        refs[-1][i] = ref[...]


def pack(parts):
    part = parts[0]
    return pl.pallas_call(
        pack_kernel,
        out_shape=jax.ShapeDtypeStruct((len(parts),) + part.shape, part.dtype),
        in_specs=[vmem()] * len(parts),
        out_specs=vmem(),
        name="pack",
        compiler_params=pltpu.CompilerParams(vmem_limit_bytes=4 << 20),
        cost_estimate=pl.CostEstimate(
            flops=0, bytes_accessed=4 * len(parts) * part.size, transcendentals=0
        ),
    )(*parts)


def on_device(calib, base_weight, keep_blocks):
    tokens = calib.shape[0] * 8
    weight, diff, keep = start(keep_blocks, base_weight)
    diff, calib = lax.optimization_barrier((diff, calib))
    diffs = lax.all_gather(diff, ROW, axis=0)

    feats = calib.T
    own = lax.all_gather(feats, "zh", axis=0, tiled=True)
    other = lax.ppermute(own, "ylo", SWAP)
    own_mate = lax.ppermute(own, "core", SWAP)
    rows = lax.all_gather(feats, "zl", axis=0, tiled=True)
    rows, other = lax.optimization_barrier((rows, other))
    other_mate = lax.ppermute(other, "core", SWAP)
    term = partial_gram(rows, own, other, own_mate, other_mate)
    terms = lax.all_to_all(term, ROW, 0, 0, tiled=True)
    diffs, terms = lax.optimization_barrier((diffs, terms))
    gram = (jnp.sum(terms.astype(jnp.float32), axis=0) / tokens).astype(jnp.bfloat16)

    line = ("zh", "zl", "core")
    mine = lax.all_to_all(jnp.broadcast_to(gram[None], (4,) + gram.shape), "zh", 0, 0, tiled=True)
    up, down, two = from_z(1, 1), from_z(-1, -1), from_z(2, -2)
    far = lax.ppermute(mine, "ylo", SWAP)
    near = [mine] + [lax.ppermute(mine, line, s) for s in (up, down, two)]
    far = [far] + [lax.ppermute(g, "ylo", SWAP) for g in near[1:3]] + [lax.ppermute(far, line, two)]
    far[1], far[3], *held = lax.optimization_barrier((far[1], far[3], *near))
    near_mate = lax.ppermute(pack(held), "core", SWAP)
    far[2], near_mate = lax.optimization_barrier((far[2], near_mate))
    far_mate = lax.ppermute(pack(far), "core", SWAP)
    grams = near + [near_mate] + far + [far_mate]

    weight, sent = step(False, diffs, grams, weight, base_weight, keep)
    diffs = lax.all_to_all(sent, ROW, 0, 0, tiled=True)
    return step(True, diffs, grams, weight, base_weight, keep)[0]


def solution(mesh):
    split = Mesh(mesh.devices.reshape(SIZES), AXES)
    return jax.shard_map(
        on_device,
        mesh=split,
        in_specs=(P(ROW, TOK), P(TOK, ROW), P()),
        out_specs=P(TOK, ROW),
        check_vma=False,
    )
```

```python
import functools

import jax
import jax.numpy as jnp
from jax import lax
from jax.experimental import pallas as pl
from jax.experimental.pallas import tpu as pltpu
from jax.sharding import Mesh, PartitionSpec as P

BLOCK = 128
RATE = 0.25
NT = (((1,), (1,)), ((), ()))
AXES = ("ylo", "zh", "zl", "core", "yhi", "x")
SIZES = (2, 4, 4, 2, 2, 4)
TOK = ("ylo", "zh", "zl", "core")
ROW = ("yhi", "x")
SWAP = ((0, 1), (1, 0))
CLASSES = (0, 1, 3, 2)


def from_z(*steps):
    return [((z + s) % 16 * 2 + c, z * 2 + c) for z in range(16) for c, s in enumerate(steps)]


def vmem():
    return pl.BlockSpec(memory_space=pltpu.VMEM)


def smem():
    return pl.BlockSpec(memory_space=pltpu.SMEM)


def by_core(x):
    chunk = BLOCK // 2
    order = [2 * i + c for c in range(2) for i in range(x.shape[1] // BLOCK)]
    return jnp.concatenate([x[:, i * chunk : (i + 1) * chunk] for i in order], axis=1)


def start_kernel(kept, base, weight, diff, keep_out):
    tok = lax.axis_index(TOK)
    first = lax.axis_index(ROW) * (base.shape[1] // BLOCK)
    block = lax.broadcasted_iota(jnp.int32, base.shape, 1) // BLOCK
    keep = jnp.zeros(base.shape, jnp.float32)
    for b in range(base.shape[1] // BLOCK):
        listed = jnp.int32(0)
        for j in range(kept.shape[0]):
            listed = jnp.where(kept[j, tok] == first + b, 1, listed)
        keep = jnp.where(block == b, listed.astype(jnp.float32), keep)
    base_float = base[...].astype(jnp.float32)
    new = (keep * base_float).astype(jnp.bfloat16)
    weight[...] = new
    keep_out[...] = keep
    diff[...] = by_core((new.astype(jnp.float32) - base_float).astype(jnp.bfloat16))


def start(keep_blocks, base):
    bf16 = jax.ShapeDtypeStruct(base.shape, base.dtype)
    return pl.pallas_call(
        start_kernel,
        out_shape=(bf16, bf16, jax.ShapeDtypeStruct(base.shape, jnp.float32)),
        in_specs=[smem(), vmem()],
        out_specs=(vmem(),) * 3,
        name="start",
        compiler_params=pltpu.CompilerParams(vmem_limit_bytes=4 << 20),
    )(keep_blocks.T, base)


def partial_gram_kernel(rows, s00, s10, s01, s11, out):
    ylo, core = lax.axis_index("ylo"), lax.axis_index("core")
    chunk = BLOCK // 2
    for dy, dc, cols in ((0, 0, s00), (1, 0, s10), (0, 1, s01), (1, 1, s11)):
        term = lax.dot_general(cols[...], rows[...], NT, preferred_element_type=jnp.float32)
        term = term.astype(jnp.bfloat16).reshape(4, chunk, rows.shape[0])
        half = pl.ds(pl.multiple_of((core ^ dc) * chunk, chunk), chunk)
        out[pl.ds((ylo ^ dy) * 4, 4), half, :] = term


def partial_gram(rows, *cols):
    k = rows.shape[0]
    return pl.pallas_call(
        partial_gram_kernel,
        out_shape=jax.ShapeDtypeStruct((8, BLOCK, k), jnp.bfloat16),
        in_specs=[vmem()] * 5,
        out_specs=vmem(),
        name="partial_gram",
        compiler_params=pltpu.CompilerParams(vmem_limit_bytes=8 << 20),
        cost_estimate=pl.CostEstimate(
            flops=8 * k * k * rows.shape[1], bytes_accessed=12 * rows.size, transcendentals=0
        ),
    )(rows, *cols)


def step_kernel(last, diffs, *refs):
    grams, (weight, base, keep), outs, total = refs[:4], refs[4:7], refs[7:-1], refs[-1]
    zl, core = lax.axis_index("zl"), lax.axis_index("core")
    half = grams[0].shape[3]
    for j, shift in enumerate(CLASSES):
        part = jnp.zeros((weight.shape[0], BLOCK), jnp.float32)
        for c in range(2):
            gram = grams[2 * c + 1].at[j - 1] if j else grams[2 * c]
            lanes = pl.ds(pl.multiple_of((core ^ c) * half, half), half)
            for h in range(4):
                for y in range(2):
                    part += lax.dot_general(
                        diffs[y * 4 + h, :, lanes], gram[h, y], NT,
                        preferred_element_type=jnp.float32,
                    )
        place = lax.rem(zl + shift, 4) * BLOCK
        total[:, pl.ds(pl.multiple_of(place, BLOCK), BLOCK)] = part
    old = weight[...].astype(jnp.float32)
    new = (old - RATE * keep[...] * total[...]).astype(jnp.bfloat16)
    outs[0][...] = new
    if not last:
        diff = (new.astype(jnp.float32) - base[...].astype(jnp.float32)).astype(jnp.bfloat16)
        diff = by_core(diff)
        for i in range(outs[1].shape[0]):
            outs[1][i] = diff


def step(last, diffs, grams, weight, base, keep):
    shape = jax.ShapeDtypeStruct(weight.shape, weight.dtype)
    outs = (shape,) if last else (shape, jax.ShapeDtypeStruct(diffs.shape, diffs.dtype))
    return pl.pallas_call(
        functools.partial(step_kernel, last),
        out_shape=outs,
        in_specs=[vmem()] * (len(grams) + 4),
        out_specs=tuple(vmem() for _ in outs),
        scratch_shapes=[pltpu.VMEM(weight.shape, jnp.float32)],
        name="last_step" if last else "first_step",
        compiler_params=pltpu.CompilerParams(vmem_limit_bytes=16 << 20),
        cost_estimate=pl.CostEstimate(
            flops=2 * diffs.size * weight.shape[1], bytes_accessed=12 * diffs.size // 2,
            transcendentals=0,
        ),
    )(diffs, *grams, weight, base, keep)


def pack_kernel(up, down, two, two_far, out):
    ylo = lax.axis_index("ylo")
    out[0] = up[...]
    out[1] = down[...]
    out[2, :, ylo] = two[...]
    out[2, :, 1 - ylo] = two_far[...]


def pack(up, *others):
    return pl.pallas_call(
        pack_kernel,
        out_shape=jax.ShapeDtypeStruct((3,) + up.shape, up.dtype),
        in_specs=[vmem()] * 4,
        out_specs=vmem(),
        name="pack",
        compiler_params=pltpu.CompilerParams(vmem_limit_bytes=4 << 20),
        cost_estimate=pl.CostEstimate(
            flops=0, bytes_accessed=12 * up.size, transcendentals=0
        ),
    )(up, *others)


def on_device(calib, base_weight, keep_blocks):
    tokens = calib.shape[0] * 8
    weight, diff, keep = start(keep_blocks, base_weight)
    diff, calib = lax.optimization_barrier((diff, calib))
    diffs = lax.all_gather(diff, ROW, axis=0)

    feats = calib.T
    own = lax.all_gather(feats, "zh", axis=0, tiled=True)
    other = lax.ppermute(own, "ylo", SWAP)
    own_mate = lax.ppermute(own, "core", SWAP)
    rows = lax.all_gather(feats, "zl", axis=0, tiled=True)
    rows, other = lax.optimization_barrier((rows, other))
    other_mate = lax.ppermute(other, "core", SWAP)
    term = partial_gram(rows, own, other, own_mate, other_mate)
    terms = lax.all_to_all(term, ROW, 0, 0, tiled=True)
    diffs, terms = lax.optimization_barrier((diffs, terms))
    gram = (jnp.sum(terms.astype(jnp.float32), axis=0) / tokens).astype(jnp.bfloat16)

    line = ("zh", "zl", "core")
    mine = lax.all_gather(lax.all_gather(gram, "ylo", axis=0), "zh", axis=0)
    half = lax.dynamic_index_in_dim(mine, lax.axis_index("ylo"), 1, keepdims=False)
    two = lax.ppermute(half, line, from_z(2, -2))
    up, down = (lax.ppermute(mine, line, from_z(s, s)) for s in (1, -1))
    mine_mate = lax.ppermute(mine, "core", SWAP)
    two_far = lax.ppermute(two, "ylo", SWAP)
    mine_mate, up = lax.optimization_barrier((mine_mate, up))
    packed = pack(up, down, two, two_far)
    packed_mate = lax.ppermute(packed, "core", SWAP)
    grams = (mine, packed, mine_mate, packed_mate)

    weight, sent = step(False, diffs, grams, weight, base_weight, keep)
    diffs = lax.all_to_all(sent, ROW, 0, 0, tiled=True)
    return step(True, diffs, grams, weight, base_weight, keep)[0]


def solution(mesh):
    split = Mesh(mesh.devices.reshape(SIZES), AXES)
    return jax.shard_map(
        on_device,
        mesh=split,
        in_specs=(P(ROW, TOK), P(TOK, ROW), P()),
        out_specs=P(TOK, ROW),
        check_vma=False,
    )
```

```python
import functools

import jax
import jax.numpy as jnp
from jax import lax
from jax.experimental import pallas as pl
from jax.experimental.pallas import tpu as pltpu
from jax.sharding import Mesh, PartitionSpec as P

BLOCK = 128
RATE = 0.25
NT = (((1,), (1,)), ((), ()))
AXES = ("ylo", "zh", "zl", "core", "yhi", "x")
SIZES = (2, 4, 4, 2, 2, 4)
TOK = ("ylo", "zh", "zl", "core")
ROW = ("yhi", "x")
SWAP = ((0, 1), (1, 0))
CLASSES = (0, 1, 3, 2)


def from_z(*steps):
    return [((z + s) % 16 * 2 + c, z * 2 + c) for z in range(16) for c, s in enumerate(steps)]


def vmem():
    return pl.BlockSpec(memory_space=pltpu.VMEM)


def smem():
    return pl.BlockSpec(memory_space=pltpu.SMEM)


def by_core(x):
    chunk = BLOCK // 2
    order = [2 * i + c for c in range(2) for i in range(x.shape[1] // BLOCK)]
    return jnp.concatenate([x[:, i * chunk : (i + 1) * chunk] for i in order], axis=1)


def start_kernel(kept, base, weight, diff, keep_out):
    tok = lax.axis_index(TOK)
    first = lax.axis_index(ROW) * (base.shape[1] // BLOCK)
    block = lax.broadcasted_iota(jnp.int32, base.shape, 1) // BLOCK
    keep = jnp.zeros(base.shape, jnp.float32)
    for b in range(base.shape[1] // BLOCK):
        listed = jnp.int32(0)
        for j in range(kept.shape[0]):
            listed = jnp.where(kept[j, tok] == first + b, 1, listed)
        keep = jnp.where(block == b, listed.astype(jnp.float32), keep)
    base_float = base[...].astype(jnp.float32)
    new = (keep * base_float).astype(jnp.bfloat16)
    weight[...] = new
    keep_out[...] = keep
    diff[...] = by_core((new.astype(jnp.float32) - base_float).astype(jnp.bfloat16))


def start(keep_blocks, base):
    bf16 = jax.ShapeDtypeStruct(base.shape, base.dtype)
    return pl.pallas_call(
        start_kernel,
        out_shape=(bf16, bf16, jax.ShapeDtypeStruct(base.shape, jnp.float32)),
        in_specs=[smem(), vmem()],
        out_specs=(vmem(),) * 3,
        name="start",
        compiler_params=pltpu.CompilerParams(vmem_limit_bytes=4 << 20),
    )(keep_blocks.T, base)


def partial_gram_kernel(r0, r1, r2, r3, s00, s10, s01, s11, out, rows):
    ylo, zl, core = (lax.axis_index(a) for a in ("ylo", "zl", "core"))
    chunk = BLOCK // 2
    for d, part in enumerate((r0, r1, r2, r3)):
        place = lax.rem(zl + d, 4) * chunk
        rows[pl.ds(pl.multiple_of(place, chunk), chunk), :] = part[...]
    for dy, dc, cols in ((0, 0, s00), (1, 0, s10), (0, 1, s01), (1, 1, s11)):
        term = lax.dot_general(cols[...], rows[...], NT, preferred_element_type=jnp.float32)
        term = term.astype(jnp.bfloat16).reshape(4, chunk, rows.shape[0])
        half = pl.ds(pl.multiple_of((core ^ dc) * chunk, chunk), chunk)
        out[pl.ds((ylo ^ dy) * 4, 4), half, :] = term


def partial_gram(rows, *cols):
    k, depth = cols[0].shape
    return pl.pallas_call(
        partial_gram_kernel,
        out_shape=jax.ShapeDtypeStruct((8, BLOCK, k), jnp.bfloat16),
        in_specs=[vmem()] * 8,
        out_specs=vmem(),
        scratch_shapes=[pltpu.VMEM((k, depth), jnp.bfloat16)],
        name="partial_gram",
        compiler_params=pltpu.CompilerParams(vmem_limit_bytes=8 << 20),
        cost_estimate=pl.CostEstimate(
            flops=8 * k * k * depth, bytes_accessed=12 * k * depth, transcendentals=0
        ),
    )(*rows, *cols)


def step_kernel(last, diffs, *refs):
    grams, (weight, base, keep), outs, total = refs[:4], refs[4:7], refs[7:-1], refs[-1]
    zl, core = lax.axis_index("zl"), lax.axis_index("core")
    half = grams[0].shape[3]
    for j, shift in enumerate(CLASSES):
        part = jnp.zeros((weight.shape[0], BLOCK), jnp.float32)
        for c in range(2):
            gram = grams[2 * c + 1].at[j - 1] if j else grams[2 * c]
            lanes = pl.ds(pl.multiple_of((core ^ c) * half, half), half)
            for h in range(4):
                for y in range(2):
                    part += lax.dot_general(
                        diffs[y * 4 + h, :, lanes], gram[h, y], NT,
                        preferred_element_type=jnp.float32,
                    )
        place = lax.rem(zl + shift, 4) * BLOCK
        total[:, pl.ds(pl.multiple_of(place, BLOCK), BLOCK)] = part
    old = weight[...].astype(jnp.float32)
    new = (old - RATE * keep[...] * total[...]).astype(jnp.bfloat16)
    outs[0][...] = new
    if not last:
        diff = (new.astype(jnp.float32) - base[...].astype(jnp.float32)).astype(jnp.bfloat16)
        diff = by_core(diff)
        for i in range(outs[1].shape[0]):
            outs[1][i] = diff


def step(last, diffs, grams, weight, base, keep):
    shape = jax.ShapeDtypeStruct(weight.shape, weight.dtype)
    outs = (shape,) if last else (shape, jax.ShapeDtypeStruct(diffs.shape, diffs.dtype))
    return pl.pallas_call(
        functools.partial(step_kernel, last),
        out_shape=outs,
        in_specs=[vmem()] * (len(grams) + 4),
        out_specs=tuple(vmem() for _ in outs),
        scratch_shapes=[pltpu.VMEM(weight.shape, jnp.float32)],
        name="last_step" if last else "first_step",
        compiler_params=pltpu.CompilerParams(vmem_limit_bytes=16 << 20),
        cost_estimate=pl.CostEstimate(
            flops=2 * diffs.size * weight.shape[1], bytes_accessed=12 * diffs.size // 2,
            transcendentals=0,
        ),
    )(diffs, *grams, weight, base, keep)


def pack_kernel(up, down, two, two_far, out):
    ylo = lax.axis_index("ylo")
    out[0] = up[...]
    out[1] = down[...]
    out[2, :, ylo] = two[...]
    out[2, :, 1 - ylo] = two_far[...]


def pack(up, *others):
    return pl.pallas_call(
        pack_kernel,
        out_shape=jax.ShapeDtypeStruct((3,) + up.shape, up.dtype),
        in_specs=[vmem()] * 4,
        out_specs=vmem(),
        name="pack",
        compiler_params=pltpu.CompilerParams(vmem_limit_bytes=4 << 20),
        cost_estimate=pl.CostEstimate(
            flops=0, bytes_accessed=12 * up.size, transcendentals=0
        ),
    )(up, *others)


def on_device(calib, base_weight, keep_blocks):
    tokens = calib.shape[0] * 8
    weight, diff, keep = start(keep_blocks, base_weight)
    diff, calib = lax.optimization_barrier((diff, calib))
    diffs = lax.all_gather(diff, ROW, axis=0)

    feats = calib.T
    own = lax.all_gather(feats, "zh", axis=0, tiled=True)
    other = lax.ppermute(own, "ylo", SWAP)
    own_mate = lax.ppermute(own, "core", SWAP)
    near = lax.optimization_barrier((feats, own))[0]
    rows = [feats] + [lax.ppermute(near, "zl", [((i + d) % 4, i) for i in range(4)]) for d in (1, 2, 3)]
    other, *rows[1:] = lax.optimization_barrier((other, *rows[1:]))
    other_mate = lax.ppermute(other, "core", SWAP)
    term = partial_gram(rows, own, other, own_mate, other_mate)
    terms = lax.all_to_all(term, ROW, 0, 0, tiled=True)
    diffs, terms = lax.optimization_barrier((diffs, terms))
    gram = (jnp.sum(terms.astype(jnp.float32), axis=0) / tokens).astype(jnp.bfloat16)

    line = ("zh", "zl", "core")
    mine = lax.all_gather(lax.all_gather(gram, "ylo", axis=0), "zh", axis=0)
    half = lax.dynamic_index_in_dim(mine, lax.axis_index("ylo"), 1, keepdims=False)
    two = lax.ppermute(half, line, from_z(2, -2))
    up, down = (lax.ppermute(mine, line, from_z(s, s)) for s in (1, -1))
    mine_mate = lax.ppermute(mine, "core", SWAP)
    two_far = lax.ppermute(two, "ylo", SWAP)
    mine_mate, two_far = lax.optimization_barrier((mine_mate, two_far))
    packed = pack(up, down, two, two_far)
    packed_mate = lax.ppermute(packed, "core", SWAP)
    grams = (mine, packed, mine_mate, packed_mate)

    weight, sent = step(False, diffs, grams, weight, base_weight, keep)
    diffs = lax.all_to_all(sent, ROW, 0, 0, tiled=True)
    return step(True, diffs, grams, weight, base_weight, keep)[0]


def solution(mesh):
    split = Mesh(mesh.devices.reshape(SIZES), AXES)
    return jax.shard_map(
        on_device,
        mesh=split,
        in_specs=(P(ROW, TOK), P(TOK, ROW), P()),
        out_specs=P(TOK, ROW),
        check_vma=False,
    )
```

```python
import functools

import jax
import jax.numpy as jnp
from jax import lax
from jax.experimental import pallas as pl
from jax.experimental.pallas import tpu as pltpu
from jax.sharding import Mesh, PartitionSpec as P

BLOCK = 128
RATE = 0.25
NT = (((1,), (1,)), ((), ()))
AXES = ("ylo", "zh", "zl", "core", "yhi", "x")
SIZES = (2, 4, 4, 2, 2, 4)
TOK = ("ylo", "zh", "zl", "core")
ROW = ("yhi", "x")
SWAP = ((0, 1), (1, 0))
CLASSES = (0, 1, 3, 2)


def from_z(*steps):
    return [((z + s) % 16 * 2 + c, z * 2 + c) for z in range(16) for c, s in enumerate(steps)]


def vmem():
    return pl.BlockSpec(memory_space=pltpu.VMEM)


def smem():
    return pl.BlockSpec(memory_space=pltpu.SMEM)


def by_core(x):
    chunk = BLOCK // 2
    order = [2 * i + c for c in range(2) for i in range(x.shape[1] // BLOCK)]
    return jnp.concatenate([x[:, i * chunk : (i + 1) * chunk] for i in order], axis=1)


def start_kernel(kept, base, weight, diff, keep_out):
    tok = lax.axis_index(TOK)
    first = lax.axis_index(ROW) * (base.shape[1] // BLOCK)
    block = lax.broadcasted_iota(jnp.int32, base.shape, 1) // BLOCK
    keep = jnp.zeros(base.shape, jnp.float32)
    for b in range(base.shape[1] // BLOCK):
        listed = jnp.int32(0)
        for j in range(kept.shape[0]):
            listed = jnp.where(kept[j, tok] == first + b, 1, listed)
        keep = jnp.where(block == b, listed.astype(jnp.float32), keep)
    base_float = base[...].astype(jnp.float32)
    new = (keep * base_float).astype(jnp.bfloat16)
    weight[...] = new
    keep_out[...] = keep
    diff[...] = by_core((new.astype(jnp.float32) - base_float).astype(jnp.bfloat16))


def start(keep_blocks, base):
    bf16 = jax.ShapeDtypeStruct(base.shape, base.dtype)
    return pl.pallas_call(
        start_kernel,
        out_shape=(bf16, bf16, jax.ShapeDtypeStruct(base.shape, jnp.float32)),
        in_specs=[smem(), vmem()],
        out_specs=(vmem(),) * 3,
        name="start",
        compiler_params=pltpu.CompilerParams(vmem_limit_bytes=4 << 20),
    )(keep_blocks.T, base)


def partial_gram_kernel(r0, r1, r2, r3, cols, mates, out, rows):
    ylo, zl, core = (lax.axis_index(a) for a in ("ylo", "zl", "core"))
    chunk = BLOCK // 2
    for d, part in enumerate((r0, r1, r2, r3)):
        place = lax.rem(zl + d, 4) * chunk
        rows[pl.ds(pl.multiple_of(place, chunk), chunk), :] = part[...]
    for dy, dc, part in ((0, 0, cols), (1, 0, cols), (0, 1, mates), (1, 1, mates)):
        term = lax.dot_general(part[dy], rows[...], NT, preferred_element_type=jnp.float32)
        term = term.astype(jnp.bfloat16).reshape(4, chunk, rows.shape[0])
        half = pl.ds(pl.multiple_of((core ^ dc) * chunk, chunk), chunk)
        out[pl.ds((ylo ^ dy) * 4, 4), half, :] = term


def partial_gram(rows, *cols):
    k, depth = cols[0].shape[1:]
    return pl.pallas_call(
        partial_gram_kernel,
        out_shape=jax.ShapeDtypeStruct((8, BLOCK, k), jnp.bfloat16),
        in_specs=[vmem()] * 6,
        out_specs=vmem(),
        scratch_shapes=[pltpu.VMEM((k, depth), jnp.bfloat16)],
        name="partial_gram",
        compiler_params=pltpu.CompilerParams(vmem_limit_bytes=8 << 20),
        cost_estimate=pl.CostEstimate(
            flops=8 * k * k * depth, bytes_accessed=12 * k * depth, transcendentals=0
        ),
    )(*rows, *cols)


def step_kernel(last, diffs, *refs):
    grams, (weight, base, keep), outs, total = refs[:2], refs[2:5], refs[5:-1], refs[-1]
    zl, core = lax.axis_index("zl"), lax.axis_index("core")
    half = grams[0].shape[4]
    for j, shift in enumerate(CLASSES):
        part = jnp.zeros((weight.shape[0], BLOCK), jnp.float32)
        for c in range(2):
            lanes = pl.ds(pl.multiple_of((core ^ c) * half, half), half)
            for h in range(4):
                for y in range(2):
                    part += lax.dot_general(
                        diffs[y * 4 + h, :, lanes], grams[c][j, h, y], NT,
                        preferred_element_type=jnp.float32,
                    )
        place = lax.rem(zl + shift, 4) * BLOCK
        total[:, pl.ds(pl.multiple_of(place, BLOCK), BLOCK)] = part
    old = weight[...].astype(jnp.float32)
    new = (old - RATE * keep[...] * total[...]).astype(jnp.bfloat16)
    outs[0][...] = new
    if not last:
        diff = (new.astype(jnp.float32) - base[...].astype(jnp.float32)).astype(jnp.bfloat16)
        diff = by_core(diff)
        for i in range(outs[1].shape[0]):
            outs[1][i] = diff


def step(last, diffs, grams, weight, base, keep):
    shape = jax.ShapeDtypeStruct(weight.shape, weight.dtype)
    outs = (shape,) if last else (shape, jax.ShapeDtypeStruct(diffs.shape, diffs.dtype))
    return pl.pallas_call(
        functools.partial(step_kernel, last),
        out_shape=outs,
        in_specs=[vmem()] * (len(grams) + 4),
        out_specs=tuple(vmem() for _ in outs),
        scratch_shapes=[pltpu.VMEM(weight.shape, jnp.float32)],
        name="last_step" if last else "first_step",
        compiler_params=pltpu.CompilerParams(vmem_limit_bytes=16 << 20),
        cost_estimate=pl.CostEstimate(
            flops=2 * diffs.size * weight.shape[1], bytes_accessed=12 * diffs.size // 2,
            transcendentals=0,
        ),
    )(diffs, *grams, weight, base, keep)


def pair_kernel(own, other, out):
    out[0] = own[...]
    out[1] = other[...]


def classes_kernel(mine, up, down, two, two_far, out):
    ylo = lax.axis_index("ylo")
    out[0] = mine[...]
    out[1] = up[...]
    out[2] = down[...]
    out[3, :, ylo] = two[...]
    out[3, :, 1 - ylo] = two_far[...]


def pack(kernel, name, *parts):
    shape = ((2 if name == "pair" else 4),) + parts[0].shape
    return pl.pallas_call(
        kernel,
        out_shape=jax.ShapeDtypeStruct(shape, parts[0].dtype),
        in_specs=[vmem()] * len(parts),
        out_specs=vmem(),
        name=name,
        compiler_params=pltpu.CompilerParams(vmem_limit_bytes=4 << 20),
        cost_estimate=pl.CostEstimate(
            flops=0, bytes_accessed=4 * shape[0] * parts[0].size, transcendentals=0
        ),
    )(*parts)


def on_device(calib, base_weight, keep_blocks):
    tokens = calib.shape[0] * 8
    feats = calib.T
    own = lax.all_gather(feats, "zh", axis=0, tiled=True)
    other = lax.ppermute(own, "ylo", SWAP)
    near = lax.optimization_barrier((feats, own))[0]
    rows = [feats] + [lax.ppermute(near, "zl", [((i + d) % 4, i) for i in range(4)]) for d in (1, 2, 3)]
    other, *rows[1:] = lax.optimization_barrier((other, *rows[1:]))
    cols = pack(pair_kernel, "pair", own, other)
    mates = lax.ppermute(cols, "core", SWAP)

    base_weight = lax.optimization_barrier((base_weight, cols))[0]
    weight, diff, keep = start(keep_blocks, base_weight)
    diff, mates = lax.optimization_barrier((diff, mates))
    diffs = lax.all_gather(diff, ROW, axis=0)

    term = partial_gram(rows, cols, mates)
    terms = lax.all_to_all(term, ROW, 0, 0, tiled=True)
    gram = (jnp.sum(terms.astype(jnp.float32), axis=0) / tokens).astype(jnp.bfloat16)

    line = ("zh", "zl", "core")
    mine = lax.all_gather(lax.all_gather(gram, "ylo", axis=0), "zh", axis=0)
    half = lax.dynamic_index_in_dim(mine, lax.axis_index("ylo"), 1, keepdims=False)
    two = lax.ppermute(half, line, from_z(2, -2))
    up, down = (lax.ppermute(mine, line, from_z(s, s)) for s in (1, -1))
    two_far = lax.ppermute(two, "ylo", SWAP)
    diffs, two_far = lax.optimization_barrier((diffs, two_far))
    packed = pack(classes_kernel, "classes", mine, up, down, two, two_far)
    grams = (packed, lax.ppermute(packed, "core", SWAP))

    weight, sent = step(False, diffs, grams, weight, base_weight, keep)
    diffs = lax.all_to_all(sent, ROW, 0, 0, tiled=True)
    return step(True, diffs, grams, weight, base_weight, keep)[0]


def solution(mesh):
    split = Mesh(mesh.devices.reshape(SIZES), AXES)
    return jax.shard_map(
        on_device,
        mesh=split,
        in_specs=(P(ROW, TOK), P(TOK, ROW), P()),
        out_specs=P(TOK, ROW),
        check_vma=False,
    )
```

```python
import functools

import jax
import jax.numpy as jnp
from jax import lax
from jax.experimental import pallas as pl
from jax.experimental.pallas import tpu as pltpu
from jax.sharding import Mesh, PartitionSpec as P

BLOCK = 128
RATE = 0.25
NT = (((1,), (1,)), ((), ()))
AXES = ("ylo", "zh", "zl", "core", "yhi", "x")
SIZES = (2, 4, 4, 2, 2, 4)
TOK = ("ylo", "zh", "zl", "core")
ROW = ("yhi", "x")
SWAP = ((0, 1), (1, 0))
CLASSES = (0, 1, 3, 2)


def from_z(*steps):
    return [((z + s) % 16 * 2 + c, z * 2 + c) for z in range(16) for c, s in enumerate(steps)]


def vmem():
    return pl.BlockSpec(memory_space=pltpu.VMEM)


def smem():
    return pl.BlockSpec(memory_space=pltpu.SMEM)


def by_core(x):
    chunk = BLOCK // 2
    order = [2 * i + c for c in range(2) for i in range(x.shape[1] // BLOCK)]
    return jnp.concatenate([x[:, i * chunk : (i + 1) * chunk] for i in order], axis=1)


def start_kernel(kept, base, weight, diff, keep_out):
    tok = lax.axis_index(TOK)
    first = lax.axis_index(ROW) * (base.shape[1] // BLOCK)
    block = lax.broadcasted_iota(jnp.int32, base.shape, 1) // BLOCK
    keep = jnp.zeros(base.shape, jnp.float32)
    for b in range(base.shape[1] // BLOCK):
        listed = jnp.int32(0)
        for j in range(kept.shape[0]):
            listed = jnp.where(kept[j, tok] == first + b, 1, listed)
        keep = jnp.where(block == b, listed.astype(jnp.float32), keep)
    base_float = base[...].astype(jnp.float32)
    new = (keep * base_float).astype(jnp.bfloat16)
    weight[...] = new
    keep_out[...] = keep
    diff[...] = by_core((new.astype(jnp.float32) - base_float).astype(jnp.bfloat16))


def start(keep_blocks, base):
    bf16 = jax.ShapeDtypeStruct(base.shape, base.dtype)
    return pl.pallas_call(
        start_kernel,
        out_shape=(bf16, bf16, jax.ShapeDtypeStruct(base.shape, jnp.float32)),
        in_specs=[smem(), vmem()],
        out_specs=(vmem(),) * 3,
        name="start",
        compiler_params=pltpu.CompilerParams(vmem_limit_bytes=4 << 20),
    )(keep_blocks.T, base)


def forward_kernel(below, above, both, onward):
    both[0] = below[...]
    both[1] = above[...]
    onward[...] = jnp.where(lax.axis_index("core") == 0, below[...], above[...])


def forward(below, above):
    shape = below.shape
    return pl.pallas_call(
        forward_kernel,
        out_shape=tuple(jax.ShapeDtypeStruct(d + shape, below.dtype) for d in ((2,), ())),
        in_specs=[vmem()] * 2,
        out_specs=(vmem(),) * 2,
        name="forward",
        compiler_params=pltpu.CompilerParams(vmem_limit_bytes=2 << 20),
        cost_estimate=pl.CostEstimate(
            flops=0, bytes_accessed=10 * below.size, transcendentals=0
        ),
    )(below, above)


def columns_kernel(*refs):
    ylo, zh, out = lax.axis_index("ylo"), lax.axis_index("zh"), refs[-1]
    for y in range(2):
        mine, both, across = refs[3 * y : 3 * y + 3]
        for d, part in ((0, mine), (3, both.at[0]), (1, both.at[1]), (2, across)):
            out[ylo ^ y, lax.rem(zh + d, 4)] = part[...]


def columns(*parts):
    shape = (2, 4) + parts[0].shape
    return pl.pallas_call(
        columns_kernel,
        out_shape=jax.ShapeDtypeStruct(shape, parts[0].dtype),
        in_specs=[vmem()] * len(parts),
        out_specs=vmem(),
        name="columns",
        compiler_params=pltpu.CompilerParams(vmem_limit_bytes=4 << 20),
        cost_estimate=pl.CostEstimate(
            flops=0, bytes_accessed=32 * parts[0].size, transcendentals=0
        ),
    )(*parts)


def partial_gram_kernel(r0, r1, r2, r3, cols, mates, out, rows):
    zl, core = lax.axis_index("zl"), lax.axis_index("core")
    chunk, depth = r0.shape
    for d, part in enumerate((r0, r1, r2, r3)):
        place = lax.rem(zl + d, 4) * chunk
        rows[pl.ds(pl.multiple_of(place, chunk), chunk), :] = part[...]
    for c, part in enumerate((cols, mates)):
        half = pl.ds(pl.multiple_of((core ^ c) * chunk, chunk), chunk)
        for y in range(2):
            term = lax.dot_general(
                part[y].reshape(4 * chunk, depth), rows[...], NT,
                preferred_element_type=jnp.float32,
            )
            term = term.astype(jnp.bfloat16).reshape(4, chunk, rows.shape[0])
            out[4 * y : 4 * y + 4, half, :] = term


def partial_gram(rows, *cols):
    chunk, depth = rows[0].shape
    k = 4 * chunk
    return pl.pallas_call(
        partial_gram_kernel,
        out_shape=jax.ShapeDtypeStruct((8, BLOCK, k), jnp.bfloat16),
        in_specs=[vmem()] * 6,
        out_specs=vmem(),
        scratch_shapes=[pltpu.VMEM((k, depth), jnp.bfloat16)],
        name="partial_gram",
        compiler_params=pltpu.CompilerParams(vmem_limit_bytes=8 << 20),
        cost_estimate=pl.CostEstimate(
            flops=8 * k * k * depth, bytes_accessed=12 * k * depth, transcendentals=0
        ),
    )(*rows, *cols)


def step_kernel(last, diffs, *refs):
    grams, (weight, base, keep), outs, total = refs[:2], refs[2:5], refs[5:-1], refs[-1]
    zl, core = lax.axis_index("zl"), lax.axis_index("core")
    half = grams[0].shape[4]
    for j, shift in enumerate(CLASSES):
        part = jnp.zeros((weight.shape[0], BLOCK), jnp.float32)
        for c in range(2):
            lanes = pl.ds(pl.multiple_of((core ^ c) * half, half), half)
            for h in range(4):
                for y in range(2):
                    part += lax.dot_general(
                        diffs[y * 4 + h, :, lanes], grams[c][j, h, y], NT,
                        preferred_element_type=jnp.float32,
                    )
        place = lax.rem(zl + shift, 4) * BLOCK
        total[:, pl.ds(pl.multiple_of(place, BLOCK), BLOCK)] = part
    old = weight[...].astype(jnp.float32)
    new = (old - RATE * keep[...] * total[...]).astype(jnp.bfloat16)
    outs[0][...] = new
    if not last:
        diff = (new.astype(jnp.float32) - base[...].astype(jnp.float32)).astype(jnp.bfloat16)
        diff = by_core(diff)
        for i in range(outs[1].shape[0]):
            outs[1][i] = diff


def step(last, diffs, grams, weight, base, keep):
    shape = jax.ShapeDtypeStruct(weight.shape, weight.dtype)
    outs = (shape,) if last else (shape, jax.ShapeDtypeStruct(diffs.shape, diffs.dtype))
    return pl.pallas_call(
        functools.partial(step_kernel, last),
        out_shape=outs,
        in_specs=[vmem()] * (len(grams) + 4),
        out_specs=tuple(vmem() for _ in outs),
        scratch_shapes=[pltpu.VMEM(weight.shape, jnp.float32)],
        name="last_step" if last else "first_step",
        compiler_params=pltpu.CompilerParams(vmem_limit_bytes=16 << 20),
        cost_estimate=pl.CostEstimate(
            flops=2 * diffs.size * weight.shape[1], bytes_accessed=12 * diffs.size // 2,
            transcendentals=0,
        ),
    )(diffs, *grams, weight, base, keep)


def classes_kernel(mine, up, down, two, two_far, out):
    ylo = lax.axis_index("ylo")
    out[0] = mine[...]
    out[1] = up[...]
    out[2] = down[...]
    out[3, :, ylo] = two[...]
    out[3, :, 1 - ylo] = two_far[...]


def pack(*parts):
    shape = (4,) + parts[0].shape
    return pl.pallas_call(
        classes_kernel,
        out_shape=jax.ShapeDtypeStruct(shape, parts[0].dtype),
        in_specs=[vmem()] * len(parts),
        out_specs=vmem(),
        name="classes",
        compiler_params=pltpu.CompilerParams(vmem_limit_bytes=4 << 20),
        cost_estimate=pl.CostEstimate(
            flops=0, bytes_accessed=4 * shape[0] * parts[0].size, transcendentals=0
        ),
    )(*parts)


def on_device(calib, base_weight, keep_blocks):
    tokens = calib.shape[0] * 8
    feats = calib.T
    line = ("zh", "zl", "core")
    below, above = (lax.ppermute(feats, line, from_z(d, d)) for d in (-4, 4))
    other = lax.ppermute(feats, "ylo", SWAP)
    near, other = lax.optimization_barrier((feats, other))
    rows = [feats] + [lax.ppermute(near, "zl", [((i + d) % 4, i) for i in range(4)]) for d in (1, 2, 3)]
    both, onward = forward(below, above)
    both, *rows[2:] = lax.optimization_barrier((both, *rows[2:]))
    across = lax.ppermute(onward, line, from_z(-4, 4))
    other_both = lax.ppermute(both, "ylo", SWAP)
    other_across = lax.ppermute(across, "ylo", SWAP)
    other_both, rows[1] = lax.optimization_barrier((other_both, rows[1]))
    cols = columns(feats, both, across, other, other_both, other_across)
    mates = lax.ppermute(cols, "core", SWAP)

    base_weight = lax.optimization_barrier((base_weight, cols))[0]
    weight, diff, keep = start(keep_blocks, base_weight)
    diff, mates = lax.optimization_barrier((diff, mates))
    diffs = lax.all_gather(diff, ROW, axis=0)

    term = partial_gram(rows, cols, mates)
    terms = lax.all_to_all(term, ROW, 0, 0, tiled=True)
    gram = (jnp.sum(terms.astype(jnp.float32), axis=0) / tokens).astype(jnp.bfloat16)

    mine = lax.all_gather(lax.all_gather(gram, "ylo", axis=0), "zh", axis=0)
    half = lax.dynamic_index_in_dim(mine, lax.axis_index("ylo"), 1, keepdims=False)
    two = lax.ppermute(half, line, from_z(2, -2))
    up, down = (lax.ppermute(mine, line, from_z(s, s)) for s in (1, -1))
    two_far = lax.ppermute(two, "ylo", SWAP)
    diffs, two_far = lax.optimization_barrier((diffs, two_far))
    packed = pack(mine, up, down, two, two_far)
    grams = (packed, lax.ppermute(packed, "core", SWAP))

    weight, sent = step(False, diffs, grams, weight, base_weight, keep)
    diffs = lax.all_to_all(sent, ROW, 0, 0, tiled=True)
    return step(True, diffs, grams, weight, base_weight, keep)[0]


def solution(mesh):
    split = Mesh(mesh.devices.reshape(SIZES), AXES)
    return jax.shard_map(
        on_device,
        mesh=split,
        in_specs=(P(ROW, TOK), P(TOK, ROW), P()),
        out_specs=P(TOK, ROW),
        check_vma=False,
    )
```

```python
import functools

import jax
import jax.numpy as jnp
from jax import lax
from jax.experimental import pallas as pl
from jax.experimental.pallas import tpu as pltpu
from jax.sharding import Mesh, PartitionSpec as P

BLOCK = 128
RATE = 0.25
NT = (((1,), (1,)), ((), ()))
AXES = ("ylo", "zh", "zl", "core", "yhi", "x")
SIZES = (2, 4, 4, 2, 2, 4)
TOK = ("ylo", "zh", "zl", "core")
ROW = ("yhi", "x")
SWAP = ((0, 1), (1, 0))
CLASSES = (0, 1, 3, 2)


def from_z(*steps):
    return [((z + s) % 16 * 2 + c, z * 2 + c) for z in range(16) for c, s in enumerate(steps)]


def vmem():
    return pl.BlockSpec(memory_space=pltpu.VMEM)


def smem():
    return pl.BlockSpec(memory_space=pltpu.SMEM)


def by_core(x):
    chunk = BLOCK // 2
    order = [2 * i + c for c in range(2) for i in range(x.shape[1] // BLOCK)]
    return jnp.concatenate([x[:, i * chunk : (i + 1) * chunk] for i in order], axis=1)


def start_kernel(kept, base, weight, diff, keep_out):
    tok = lax.axis_index(TOK)
    first = lax.axis_index(ROW) * (base.shape[1] // BLOCK)
    block = lax.broadcasted_iota(jnp.int32, base.shape, 1) // BLOCK
    keep = jnp.zeros(base.shape, jnp.float32)
    for b in range(base.shape[1] // BLOCK):
        listed = jnp.int32(0)
        for j in range(kept.shape[0]):
            listed = jnp.where(kept[j, tok] == first + b, 1, listed)
        keep = jnp.where(block == b, listed.astype(jnp.float32), keep)
    base_float = base[...].astype(jnp.float32)
    new = (keep * base_float).astype(jnp.bfloat16)
    weight[...] = new
    keep_out[...] = keep
    sent = by_core((new.astype(jnp.float32) - base_float).astype(jnp.bfloat16))
    for i in range(diff.shape[0]):
        diff[i] = sent


def start(keep_blocks, base):
    bf16 = jax.ShapeDtypeStruct(base.shape, base.dtype)
    return pl.pallas_call(
        start_kernel,
        out_shape=(
            bf16,
            jax.ShapeDtypeStruct((8,) + base.shape, base.dtype),
            jax.ShapeDtypeStruct(base.shape, jnp.float32),
        ),
        in_specs=[smem(), vmem()],
        out_specs=(vmem(),) * 3,
        name="start",
        compiler_params=pltpu.CompilerParams(vmem_limit_bytes=4 << 20),
    )(keep_blocks.T, base)


def partial_gram_kernel(r0, r1, r2, r3, cols, mates, out, rows):
    ylo, zl, core = (lax.axis_index(a) for a in ("ylo", "zl", "core"))
    chunk = BLOCK // 2
    for d, part in enumerate((r0, r1, r2, r3)):
        place = lax.rem(zl + d, 4) * chunk
        rows[pl.ds(pl.multiple_of(place, chunk), chunk), :] = part[...]
    for dy, dc, part in ((0, 0, cols), (1, 0, cols), (0, 1, mates), (1, 1, mates)):
        term = lax.dot_general(part[dy], rows[...], NT, preferred_element_type=jnp.float32)
        term = term.astype(jnp.bfloat16).reshape(4, chunk, rows.shape[0])
        half = pl.ds(pl.multiple_of((core ^ dc) * chunk, chunk), chunk)
        out[pl.ds((ylo ^ dy) * 4, 4), half, :] = term


def partial_gram(rows, *cols):
    k, depth = cols[0].shape[1:]
    return pl.pallas_call(
        partial_gram_kernel,
        out_shape=jax.ShapeDtypeStruct((8, BLOCK, k), jnp.bfloat16),
        in_specs=[vmem()] * 6,
        out_specs=vmem(),
        scratch_shapes=[pltpu.VMEM((k, depth), jnp.bfloat16)],
        name="partial_gram",
        compiler_params=pltpu.CompilerParams(vmem_limit_bytes=8 << 20),
        cost_estimate=pl.CostEstimate(
            flops=8 * k * k * depth, bytes_accessed=12 * k * depth, transcendentals=0
        ),
    )(*rows, *cols)


def step_kernel(last, diffs, *refs):
    grams, (weight, base, keep), outs, total = refs[:2], refs[2:5], refs[5:-1], refs[-1]
    zl, core = lax.axis_index("zl"), lax.axis_index("core")
    half = grams[0].shape[4]
    for j, shift in enumerate(CLASSES):
        part = jnp.zeros((weight.shape[0], BLOCK), jnp.float32)
        for c in range(2):
            lanes = pl.ds(pl.multiple_of((core ^ c) * half, half), half)
            for h in range(4):
                for y in range(2):
                    part += lax.dot_general(
                        diffs[y * 4 + h, :, lanes], grams[c][j, h, y], NT,
                        preferred_element_type=jnp.float32,
                    )
        place = lax.rem(zl + shift, 4) * BLOCK
        total[:, pl.ds(pl.multiple_of(place, BLOCK), BLOCK)] = part
    old = weight[...].astype(jnp.float32)
    new = (old - RATE * keep[...] * total[...]).astype(jnp.bfloat16)
    outs[0][...] = new
    if not last:
        diff = (new.astype(jnp.float32) - base[...].astype(jnp.float32)).astype(jnp.bfloat16)
        diff = by_core(diff)
        for i in range(outs[1].shape[0]):
            outs[1][i] = diff


def step(last, diffs, grams, weight, base, keep):
    shape = jax.ShapeDtypeStruct(weight.shape, weight.dtype)
    outs = (shape,) if last else (shape, jax.ShapeDtypeStruct(diffs.shape, diffs.dtype))
    return pl.pallas_call(
        functools.partial(step_kernel, last),
        out_shape=outs,
        in_specs=[vmem()] * (len(grams) + 4),
        out_specs=tuple(vmem() for _ in outs),
        scratch_shapes=[pltpu.VMEM(weight.shape, jnp.float32)],
        name="last_step" if last else "first_step",
        compiler_params=pltpu.CompilerParams(vmem_limit_bytes=16 << 20),
        cost_estimate=pl.CostEstimate(
            flops=2 * diffs.size * weight.shape[1], bytes_accessed=12 * diffs.size // 2,
            transcendentals=0,
        ),
    )(diffs, *grams, weight, base, keep)


def pair_kernel(own, other, out):
    out[0] = own[...]
    out[1] = other[...]


def classes_kernel(mine, up, down, two, two_far, out):
    ylo = lax.axis_index("ylo")
    out[0] = mine[...]
    out[1] = up[...]
    out[2] = down[...]
    out[3, :, ylo] = two[...]
    out[3, :, 1 - ylo] = two_far[...]


def pack(kernel, name, *parts):
    shape = ((2 if name == "pair" else 4),) + parts[0].shape
    return pl.pallas_call(
        kernel,
        out_shape=jax.ShapeDtypeStruct(shape, parts[0].dtype),
        in_specs=[vmem()] * len(parts),
        out_specs=vmem(),
        name=name,
        compiler_params=pltpu.CompilerParams(vmem_limit_bytes=4 << 20),
        cost_estimate=pl.CostEstimate(
            flops=0, bytes_accessed=4 * shape[0] * parts[0].size, transcendentals=0
        ),
    )(*parts)


def on_device(calib, base_weight, keep_blocks):
    tokens = calib.shape[0] * 8
    feats = calib.T
    own = lax.all_gather(feats, "zh", axis=0, tiled=True)
    other = lax.ppermute(own, "ylo", SWAP)
    near = lax.optimization_barrier((feats, own))[0]
    rows = [feats] + [lax.ppermute(near, "zl", [((i + d) % 4, i) for i in range(4)]) for d in (1, 2, 3)]
    other, *rows[1:] = lax.optimization_barrier((other, *rows[1:]))
    cols = pack(pair_kernel, "pair", own, other)
    mates = lax.ppermute(cols, "core", SWAP)

    base_weight = lax.optimization_barrier((base_weight, cols))[0]
    weight, diff, keep = start(keep_blocks, base_weight)
    diff, mates = lax.optimization_barrier((diff, mates))
    term = partial_gram(rows, cols, mates)
    terms = lax.all_to_all(term, ROW, 0, 0, tiled=True)
    gram = (jnp.sum(terms.astype(jnp.float32), axis=0) / tokens).astype(jnp.bfloat16)

    line = ("zh", "zl", "core")
    mine = lax.all_gather(lax.all_gather(gram, "ylo", axis=0), "zh", axis=0)
    half = lax.dynamic_index_in_dim(mine, lax.axis_index("ylo"), 1, keepdims=False)
    two = lax.ppermute(half, line, from_z(2, -2))
    up, down = (lax.ppermute(mine, line, from_z(s, s)) for s in (1, -1))
    two_far = lax.ppermute(two, "ylo", SWAP)
    diff = lax.optimization_barrier((diff, mine))[0]
    diffs = lax.all_to_all(diff, ROW, 0, 0, tiled=True)
    diffs, two_far = lax.optimization_barrier((diffs, two_far))
    packed = pack(classes_kernel, "classes", mine, up, down, two, two_far)
    grams = (packed, lax.ppermute(packed, "core", SWAP))

    weight, sent = step(False, diffs, grams, weight, base_weight, keep)
    diffs = lax.all_to_all(sent, ROW, 0, 0, tiled=True)
    return step(True, diffs, grams, weight, base_weight, keep)[0]


def solution(mesh):
    split = Mesh(mesh.devices.reshape(SIZES), AXES)
    return jax.shard_map(
        on_device,
        mesh=split,
        in_specs=(P(ROW, TOK), P(TOK, ROW), P()),
        out_specs=P(TOK, ROW),
        check_vma=False,
    )
```

```python
import functools

import jax
import jax.numpy as jnp
from jax import lax
from jax.experimental import pallas as pl
from jax.experimental.pallas import tpu as pltpu
from jax.sharding import Mesh, PartitionSpec as P

BLOCK = 128
RATE = 0.25
NT = (((1,), (1,)), ((), ()))
AXES = ("ylo", "zh", "zl", "core", "yhi", "x")
SIZES = (2, 4, 4, 2, 2, 4)
TOK = ("ylo", "zh", "zl", "core")
ROW = ("yhi", "x")
SWAP = ((0, 1), (1, 0))
CLASSES = (0, 1, 3, 2)


def from_z(*steps):
    return [((z + s) % 16 * 2 + c, z * 2 + c) for z in range(16) for c, s in enumerate(steps)]


def vmem():
    return pl.BlockSpec(memory_space=pltpu.VMEM)


def smem():
    return pl.BlockSpec(memory_space=pltpu.SMEM)


def by_core(x):
    chunk = BLOCK // 2
    order = [2 * i + c for c in range(2) for i in range(x.shape[1] // BLOCK)]
    return jnp.concatenate([x[:, i * chunk : (i + 1) * chunk] for i in order], axis=1)


def start_kernel(kept, base, weight, diff, keep_out):
    tok = lax.axis_index(TOK)
    first = lax.axis_index(ROW) * (base.shape[1] // BLOCK)
    block = lax.broadcasted_iota(jnp.int32, base.shape, 1) // BLOCK
    keep = jnp.zeros(base.shape, jnp.float32)
    for b in range(base.shape[1] // BLOCK):
        listed = jnp.int32(0)
        for j in range(kept.shape[0]):
            listed = jnp.where(kept[j, tok] == first + b, 1, listed)
        keep = jnp.where(block == b, listed.astype(jnp.float32), keep)
    base_float = base[...].astype(jnp.float32)
    new = (keep * base_float).astype(jnp.bfloat16)
    weight[...] = new
    keep_out[...] = keep
    sent = by_core((new.astype(jnp.float32) - base_float).astype(jnp.bfloat16))
    for i in range(diff.shape[0]):
        diff[i] = sent


def start(keep_blocks, base):
    bf16 = jax.ShapeDtypeStruct(base.shape, base.dtype)
    return pl.pallas_call(
        start_kernel,
        out_shape=(
            bf16,
            jax.ShapeDtypeStruct((8,) + base.shape, base.dtype),
            jax.ShapeDtypeStruct(base.shape, jnp.float32),
        ),
        in_specs=[smem(), vmem()],
        out_specs=(vmem(),) * 3,
        name="start",
        compiler_params=pltpu.CompilerParams(vmem_limit_bytes=4 << 20),
    )(keep_blocks.T, base)


def partial_gram_kernel(r1, r2, r3, cols, mates, out, rows):
    ylo, zh, zl, core = (lax.axis_index(a) for a in TOK)
    chunk = BLOCK // 2
    mine = cols[0, pl.ds(pl.multiple_of(zh * chunk, chunk), chunk), :]
    for d, part in enumerate((mine, r1, r2, r3)):
        place = lax.rem(zl + d, 4) * chunk
        rows[pl.ds(pl.multiple_of(place, chunk), chunk), :] = part[...]
    for dy, dc, part in ((0, 0, cols), (1, 0, cols), (0, 1, mates), (1, 1, mates)):
        term = lax.dot_general(part[dy], rows[...], NT, preferred_element_type=jnp.float32)
        term = term.astype(jnp.bfloat16).reshape(4, chunk, rows.shape[0])
        half = pl.ds(pl.multiple_of((core ^ dc) * chunk, chunk), chunk)
        out[pl.ds((ylo ^ dy) * 4, 4), half, :] = term


def partial_gram(rows, *cols):
    k, depth = cols[0].shape[1:]
    return pl.pallas_call(
        partial_gram_kernel,
        out_shape=jax.ShapeDtypeStruct((8, BLOCK, k), jnp.bfloat16),
        in_specs=[vmem()] * 5,
        out_specs=vmem(),
        scratch_shapes=[pltpu.VMEM((k, depth), jnp.bfloat16)],
        name="partial_gram",
        compiler_params=pltpu.CompilerParams(vmem_limit_bytes=8 << 20),
        cost_estimate=pl.CostEstimate(
            flops=8 * k * k * depth, bytes_accessed=12 * k * depth, transcendentals=0
        ),
    )(*rows, *cols)


def step_kernel(last, diffs, *refs):
    grams, (weight, base, keep), outs, total = refs[:2], refs[2:5], refs[5:-1], refs[-1]
    zl, core = lax.axis_index("zl"), lax.axis_index("core")
    half = grams[0].shape[4]
    for j, shift in enumerate(CLASSES):
        part = jnp.zeros((weight.shape[0], BLOCK), jnp.float32)
        for c in range(2):
            lanes = pl.ds(pl.multiple_of((core ^ c) * half, half), half)
            for h in range(4):
                for y in range(2):
                    part += lax.dot_general(
                        diffs[y * 4 + h, :, lanes], grams[c][j, h, y], NT,
                        preferred_element_type=jnp.float32,
                    )
        place = lax.rem(zl + shift, 4) * BLOCK
        total[:, pl.ds(pl.multiple_of(place, BLOCK), BLOCK)] = part
    old = weight[...].astype(jnp.float32)
    new = (old - RATE * keep[...] * total[...]).astype(jnp.bfloat16)
    outs[0][...] = new
    if not last:
        diff = (new.astype(jnp.float32) - base[...].astype(jnp.float32)).astype(jnp.bfloat16)
        diff = by_core(diff)
        for i in range(outs[1].shape[0]):
            outs[1][i] = diff


def step(last, diffs, grams, weight, base, keep):
    shape = jax.ShapeDtypeStruct(weight.shape, weight.dtype)
    outs = (shape,) if last else (shape, jax.ShapeDtypeStruct(diffs.shape, diffs.dtype))
    return pl.pallas_call(
        functools.partial(step_kernel, last),
        out_shape=outs,
        in_specs=[vmem()] * (len(grams) + 4),
        out_specs=tuple(vmem() for _ in outs),
        scratch_shapes=[pltpu.VMEM(weight.shape, jnp.float32)],
        name="last_step" if last else "first_step",
        compiler_params=pltpu.CompilerParams(vmem_limit_bytes=16 << 20),
        cost_estimate=pl.CostEstimate(
            flops=2 * diffs.size * weight.shape[1], bytes_accessed=12 * diffs.size // 2,
            transcendentals=0,
        ),
    )(diffs, *grams, weight, base, keep)


def pair_kernel(own, other, out):
    out[0] = own[...]
    out[1] = other[...]


def classes_kernel(mine, up, down, two, two_far, out):
    ylo = lax.axis_index("ylo")
    out[0] = mine[...]
    out[1] = up[...]
    out[2] = down[...]
    out[3, :, ylo] = two[...]
    out[3, :, 1 - ylo] = two_far[...]


def pack(kernel, name, *parts):
    shape = ((2 if name == "pair" else 4),) + parts[0].shape
    return pl.pallas_call(
        kernel,
        out_shape=jax.ShapeDtypeStruct(shape, parts[0].dtype),
        in_specs=[vmem()] * len(parts),
        out_specs=vmem(),
        name=name,
        compiler_params=pltpu.CompilerParams(vmem_limit_bytes=4 << 20),
        cost_estimate=pl.CostEstimate(
            flops=0, bytes_accessed=4 * shape[0] * parts[0].size, transcendentals=0
        ),
    )(*parts)


def on_device(calib, base_weight, keep_blocks):
    tokens = calib.shape[0] * 8
    feats = calib.T
    own = lax.all_gather(feats, "zh", axis=0, tiled=True)
    other = lax.ppermute(own, "ylo", SWAP)
    near = lax.optimization_barrier((feats, own))[0]
    rows = [lax.ppermute(near, "zl", [((i + d) % 4, i) for i in range(4)]) for d in (1, 2, 3)]
    other, *rows = lax.optimization_barrier((other, *rows))
    cols = pack(pair_kernel, "pair", own, other)
    mates = lax.ppermute(cols, "core", SWAP)

    base_weight = lax.optimization_barrier((base_weight, cols))[0]
    weight, diff, keep = start(keep_blocks, base_weight)
    diff, mates = lax.optimization_barrier((diff, mates))
    term = partial_gram(rows, cols, mates)
    diff, term = lax.optimization_barrier((diff, term))
    terms = lax.all_to_all(term, ROW, 0, 0, tiled=True)
    diffs = lax.all_to_all(diff, ROW, 0, 0, tiled=True)
    gram = (jnp.sum(terms.astype(jnp.float32), axis=0) / tokens).astype(jnp.bfloat16)

    line = ("zh", "zl", "core")
    mine = lax.all_gather(lax.all_gather(gram, "ylo", axis=0), "zh", axis=0)
    half = lax.dynamic_index_in_dim(mine, lax.axis_index("ylo"), 1, keepdims=False)
    two = lax.ppermute(half, line, from_z(2, -2))
    up, down = (lax.ppermute(mine, line, from_z(s, s)) for s in (1, -1))
    two_far = lax.ppermute(two, "ylo", SWAP)
    diffs, two_far = lax.optimization_barrier((diffs, two_far))
    packed = pack(classes_kernel, "classes", mine, up, down, two, two_far)
    grams = (packed, lax.ppermute(packed, "core", SWAP))

    weight, sent = step(False, diffs, grams, weight, base_weight, keep)
    diffs = lax.all_to_all(sent, ROW, 0, 0, tiled=True)
    return step(True, diffs, grams, weight, base_weight, keep)[0]


def solution(mesh):
    split = Mesh(mesh.devices.reshape(SIZES), AXES)
    return jax.shard_map(
        on_device,
        mesh=split,
        in_specs=(P(ROW, TOK), P(TOK, ROW), P()),
        out_specs=P(TOK, ROW),
        check_vma=False,
    )
```

```python
import functools

import jax
import jax.numpy as jnp
from jax import lax
from jax.experimental import pallas as pl
from jax.experimental.pallas import tpu as pltpu
from jax.sharding import Mesh, PartitionSpec as P

BLOCK = 128
RATE = 0.25
NT = (((1,), (1,)), ((), ()))
AXES = ("ylo", "zh", "zl", "core", "yhi", "x")
SIZES = (2, 4, 4, 2, 2, 4)
TOK = ("ylo", "zh", "zl", "core")
ROW = ("yhi", "x")
SWAP = ((0, 1), (1, 0))
CLASSES = (0, 1, 3, 2)


def from_z(*steps):
    return [((z + s) % 16 * 2 + c, z * 2 + c) for z in range(16) for c, s in enumerate(steps)]


def vmem():
    return pl.BlockSpec(memory_space=pltpu.VMEM)


def smem():
    return pl.BlockSpec(memory_space=pltpu.SMEM)


def by_core(x):
    chunk = BLOCK // 2
    order = [2 * i + c for c in range(2) for i in range(x.shape[1] // BLOCK)]
    return jnp.concatenate([x[:, i * chunk : (i + 1) * chunk] for i in order], axis=1)


def start_kernel(kept, base, weight, diff, keep_out):
    tok = lax.axis_index(TOK)
    first = lax.axis_index(ROW) * (base.shape[1] // BLOCK)
    block = lax.broadcasted_iota(jnp.int32, base.shape, 1) // BLOCK
    keep = jnp.zeros(base.shape, jnp.float32)
    for b in range(base.shape[1] // BLOCK):
        listed = jnp.int32(0)
        for j in range(kept.shape[0]):
            listed = jnp.where(kept[j, tok] == first + b, 1, listed)
        keep = jnp.where(block == b, listed.astype(jnp.float32), keep)
    base_float = base[...].astype(jnp.float32)
    new = (keep * base_float).astype(jnp.bfloat16)
    weight[...] = new
    keep_out[...] = keep
    sent = by_core((new.astype(jnp.float32) - base_float).astype(jnp.bfloat16))
    for i in range(diff.shape[0]):
        diff[i] = sent


def start(keep_blocks, base):
    bf16 = jax.ShapeDtypeStruct(base.shape, base.dtype)
    return pl.pallas_call(
        start_kernel,
        out_shape=(
            bf16,
            jax.ShapeDtypeStruct((8,) + base.shape, base.dtype),
            jax.ShapeDtypeStruct(base.shape, jnp.float32),
        ),
        in_specs=[smem(), vmem()],
        out_specs=(vmem(),) * 3,
        name="start",
        compiler_params=pltpu.CompilerParams(vmem_limit_bytes=4 << 20),
    )(keep_blocks.T, base)


def partial_gram_kernel(r0, r1, r2, r3, cols, mates, out, rows):
    ylo, zl, core = (lax.axis_index(a) for a in ("ylo", "zl", "core"))
    chunk = BLOCK // 2
    for d, part in enumerate((r0, r1, r2, r3)):
        place = lax.rem(zl + d, 4) * chunk
        rows[pl.ds(pl.multiple_of(place, chunk), chunk), :] = part[...]
    for dy, dc, part in ((0, 0, cols), (1, 0, cols), (0, 1, mates), (1, 1, mates)):
        term = lax.dot_general(part[dy], rows[...], NT, preferred_element_type=jnp.float32)
        term = term.astype(jnp.bfloat16).reshape(4, chunk, rows.shape[0])
        half = pl.ds(pl.multiple_of((core ^ dc) * chunk, chunk), chunk)
        out[pl.ds((ylo ^ dy) * 4, 4), half, :] = term


def partial_gram(rows, *cols):
    k, depth = cols[0].shape[1:]
    return pl.pallas_call(
        partial_gram_kernel,
        out_shape=jax.ShapeDtypeStruct((8, BLOCK, k), jnp.bfloat16),
        in_specs=[vmem()] * 6,
        out_specs=vmem(),
        scratch_shapes=[pltpu.VMEM((k, depth), jnp.bfloat16)],
        name="partial_gram",
        compiler_params=pltpu.CompilerParams(vmem_limit_bytes=8 << 20),
        cost_estimate=pl.CostEstimate(
            flops=8 * k * k * depth, bytes_accessed=12 * k * depth, transcendentals=0
        ),
    )(*rows, *cols)


def step_kernel(last, diffs, *refs):
    grams, (weight, base, keep), outs, total = refs[:2], refs[2:5], refs[5:-1], refs[-1]
    zl, core = lax.axis_index("zl"), lax.axis_index("core")
    half = grams[0].shape[4]
    for j, shift in enumerate(CLASSES):
        part = jnp.zeros((weight.shape[0], BLOCK), jnp.float32)
        for c in range(2):
            lanes = pl.ds(pl.multiple_of((core ^ c) * half, half), half)
            for h in range(4):
                for y in range(2):
                    part += lax.dot_general(
                        diffs[y * 4 + h, :, lanes], grams[c][j, h, y], NT,
                        preferred_element_type=jnp.float32,
                    )
        place = lax.rem(zl + shift, 4) * BLOCK
        total[:, pl.ds(pl.multiple_of(place, BLOCK), BLOCK)] = part
    old = weight[...].astype(jnp.float32)
    new = (old - RATE * keep[...] * total[...]).astype(jnp.bfloat16)
    outs[0][...] = new
    if not last:
        diff = (new.astype(jnp.float32) - base[...].astype(jnp.float32)).astype(jnp.bfloat16)
        diff = by_core(diff)
        for i in range(outs[1].shape[0]):
            outs[1][i] = diff


def step(last, diffs, grams, weight, base, keep):
    shape = jax.ShapeDtypeStruct(weight.shape, weight.dtype)
    outs = (shape,) if last else (shape, jax.ShapeDtypeStruct(diffs.shape, diffs.dtype))
    return pl.pallas_call(
        functools.partial(step_kernel, last),
        out_shape=outs,
        in_specs=[vmem()] * (len(grams) + 4),
        out_specs=tuple(vmem() for _ in outs),
        scratch_shapes=[pltpu.VMEM(weight.shape, jnp.float32)],
        name="last_step" if last else "first_step",
        compiler_params=pltpu.CompilerParams(vmem_limit_bytes=16 << 20),
        cost_estimate=pl.CostEstimate(
            flops=2 * diffs.size * weight.shape[1], bytes_accessed=12 * diffs.size // 2,
            transcendentals=0,
        ),
    )(diffs, *grams, weight, base, keep)


def pair_kernel(own, other, out):
    out[0] = own[...]
    out[1] = other[...]


def classes_kernel(mine, up, down, two, two_far, out):
    ylo = lax.axis_index("ylo")
    out[0] = mine[...]
    out[1] = up[...]
    out[2] = down[...]
    out[3, :, ylo] = two[...]
    out[3, :, 1 - ylo] = two_far[...]


def pack(kernel, name, *parts):
    shape = ((2 if name == "pair" else 4),) + parts[0].shape
    return pl.pallas_call(
        kernel,
        out_shape=jax.ShapeDtypeStruct(shape, parts[0].dtype),
        in_specs=[vmem()] * len(parts),
        out_specs=vmem(),
        name=name,
        compiler_params=pltpu.CompilerParams(vmem_limit_bytes=4 << 20),
        cost_estimate=pl.CostEstimate(
            flops=0, bytes_accessed=4 * shape[0] * parts[0].size, transcendentals=0
        ),
    )(*parts)


def on_device(calib, base_weight, keep_blocks):
    tokens = calib.shape[0] * 8
    feats = calib.T
    own = lax.all_gather(feats, "zh", axis=0, tiled=True)
    other = lax.ppermute(own, "ylo", SWAP)
    near = lax.optimization_barrier((feats, own))[0]
    rows = [feats] + [lax.ppermute(near, "zl", [((i + d) % 4, i) for i in range(4)]) for d in (1, 2, 3)]
    other, *rows[1:] = lax.optimization_barrier((other, *rows[1:]))
    cols = pack(pair_kernel, "pair", own, other)
    mates = lax.ppermute(cols, "core", SWAP)

    base_weight = lax.optimization_barrier((base_weight, cols))[0]
    weight, diff, keep = start(keep_blocks, base_weight)
    diff, mates = lax.optimization_barrier((diff, mates))
    term = partial_gram(rows, cols, mates)
    terms = lax.all_to_all(term, ROW, 0, 0, tiled=True)
    gram = (jnp.sum(terms.astype(jnp.float32), axis=0) / tokens).astype(jnp.bfloat16)

    line = ("zh", "zl", "core")
    gram = lax.all_gather(gram, "ylo", axis=0)
    diff = lax.optimization_barrier((diff, gram))[0]
    diffs = lax.all_to_all(diff, ROW, 0, 0, tiled=True)
    mine = lax.all_gather(gram, "zh", axis=0)
    diffs, mine = lax.optimization_barrier((diffs, mine))
    half = lax.dynamic_index_in_dim(mine, lax.axis_index("ylo"), 1, keepdims=False)
    two = lax.ppermute(half, line, from_z(2, -2))
    up, down = (lax.ppermute(mine, line, from_z(s, s)) for s in (1, -1))
    two_far = lax.ppermute(two, "ylo", SWAP)
    packed = pack(classes_kernel, "classes", mine, up, down, two, two_far)
    grams = (packed, lax.ppermute(packed, "core", SWAP))

    weight, sent = step(False, diffs, grams, weight, base_weight, keep)
    diffs = lax.all_to_all(sent, ROW, 0, 0, tiled=True)
    return step(True, diffs, grams, weight, base_weight, keep)[0]


def solution(mesh):
    split = Mesh(mesh.devices.reshape(SIZES), AXES)
    return jax.shard_map(
        on_device,
        mesh=split,
        in_specs=(P(ROW, TOK), P(TOK, ROW), P()),
        out_specs=P(TOK, ROW),
        check_vma=False,
    )
```

```python
import functools

import jax
import jax.numpy as jnp
from jax import lax
from jax.experimental import pallas as pl
from jax.experimental.pallas import tpu as pltpu
from jax.sharding import Mesh, PartitionSpec as P

BLOCK = 128
RATE = 0.25
NT = (((1,), (1,)), ((), ()))
AXES = ("ylo", "zh", "zl", "core", "yhi", "x")
SIZES = (2, 4, 4, 2, 2, 4)
TOK = ("ylo", "zh", "zl", "core")
ROW = ("yhi", "x")
SWAP = ((0, 1), (1, 0))
CLASSES = (0, 1, 3, 2)


def from_z(*steps):
    return [((z + s) % 16 * 2 + c, z * 2 + c) for z in range(16) for c, s in enumerate(steps)]


def vmem():
    return pl.BlockSpec(memory_space=pltpu.VMEM)


def smem():
    return pl.BlockSpec(memory_space=pltpu.SMEM)


def by_core(x):
    chunk = BLOCK // 2
    order = [2 * i + c for c in range(2) for i in range(x.shape[1] // BLOCK)]
    return jnp.concatenate([x[:, i * chunk : (i + 1) * chunk] for i in order], axis=1)


def start_kernel(kept, base, weight, diff, keep_out):
    tok = lax.axis_index(TOK)
    first = lax.axis_index(ROW) * (base.shape[1] // BLOCK)
    block = lax.broadcasted_iota(jnp.int32, base.shape, 1) // BLOCK
    keep = jnp.zeros(base.shape, jnp.float32)
    for b in range(base.shape[1] // BLOCK):
        listed = jnp.int32(0)
        for j in range(kept.shape[0]):
            listed = jnp.where(kept[j, tok] == first + b, 1, listed)
        keep = jnp.where(block == b, listed.astype(jnp.float32), keep)
    base_float = base[...].astype(jnp.float32)
    new = (keep * base_float).astype(jnp.bfloat16)
    weight[...] = new
    keep_out[...] = keep
    sent = by_core((new.astype(jnp.float32) - base_float).astype(jnp.bfloat16))
    for i in range(diff.shape[0]):
        diff[i] = sent


def start(keep_blocks, base):
    bf16 = jax.ShapeDtypeStruct(base.shape, base.dtype)
    return pl.pallas_call(
        start_kernel,
        out_shape=(
            bf16,
            jax.ShapeDtypeStruct((8,) + base.shape, base.dtype),
            jax.ShapeDtypeStruct(base.shape, jnp.float32),
        ),
        in_specs=[smem(), vmem()],
        out_specs=(vmem(),) * 3,
        name="start",
        compiler_params=pltpu.CompilerParams(vmem_limit_bytes=4 << 20),
    )(keep_blocks.T, base)


def partial_gram_kernel(r0, r1, r2, r3, cols, mates, out, rows):
    ylo, zl, core = (lax.axis_index(a) for a in ("ylo", "zl", "core"))
    chunk = BLOCK // 2
    for d, part in enumerate((r0, r1, r2, r3)):
        place = lax.rem(zl + d, 4) * chunk
        rows[pl.ds(pl.multiple_of(place, chunk), chunk), :] = part[...]
    for dy, dc, part in ((0, 0, cols), (1, 0, cols), (0, 1, mates), (1, 1, mates)):
        term = lax.dot_general(part[dy], rows[...], NT, preferred_element_type=jnp.float32)
        term = term.astype(jnp.bfloat16).reshape(4, chunk, rows.shape[0])
        half = pl.ds(pl.multiple_of((core ^ dc) * chunk, chunk), chunk)
        out[pl.ds((ylo ^ dy) * 4, 4), half, :] = term


def partial_gram(rows, *cols):
    k, depth = cols[0].shape[1:]
    return pl.pallas_call(
        partial_gram_kernel,
        out_shape=jax.ShapeDtypeStruct((8, BLOCK, k), jnp.bfloat16),
        in_specs=[vmem()] * 6,
        out_specs=vmem(),
        scratch_shapes=[pltpu.VMEM((k, depth), jnp.bfloat16)],
        name="partial_gram",
        compiler_params=pltpu.CompilerParams(vmem_limit_bytes=8 << 20),
        cost_estimate=pl.CostEstimate(
            flops=8 * k * k * depth, bytes_accessed=12 * k * depth, transcendentals=0
        ),
    )(*rows, *cols)


def step_kernel(last, diffs, *refs):
    grams, (weight, base, keep), outs, total = refs[:2], refs[2:5], refs[5:-1], refs[-1]
    ylo, zl, core = (lax.axis_index(a) for a in ("ylo", "zl", "core"))
    half = grams[0].shape[4]
    for j, shift in enumerate(CLASSES):
        part = jnp.zeros((weight.shape[0], BLOCK), jnp.float32)
        for c in range(2):
            lanes = pl.ds(pl.multiple_of((core ^ c) * half, half), half)
            for h in range(4):
                for y in range(2):
                    part += lax.dot_general(
                        diffs[(ylo ^ y) * 4 + h, :, lanes], grams[c][j, h, y], NT,
                        preferred_element_type=jnp.float32,
                    )
        place = lax.rem(zl + shift, 4) * BLOCK
        total[:, pl.ds(pl.multiple_of(place, BLOCK), BLOCK)] = part
    old = weight[...].astype(jnp.float32)
    new = (old - RATE * keep[...] * total[...]).astype(jnp.bfloat16)
    outs[0][...] = new
    if not last:
        diff = (new.astype(jnp.float32) - base[...].astype(jnp.float32)).astype(jnp.bfloat16)
        diff = by_core(diff)
        for i in range(outs[1].shape[0]):
            outs[1][i] = diff


def step(last, diffs, grams, weight, base, keep):
    shape = jax.ShapeDtypeStruct(weight.shape, weight.dtype)
    outs = (shape,) if last else (shape, jax.ShapeDtypeStruct(diffs.shape, diffs.dtype))
    return pl.pallas_call(
        functools.partial(step_kernel, last),
        out_shape=outs,
        in_specs=[vmem()] * (len(grams) + 4),
        out_specs=tuple(vmem() for _ in outs),
        scratch_shapes=[pltpu.VMEM(weight.shape, jnp.float32)],
        name="last_step" if last else "first_step",
        compiler_params=pltpu.CompilerParams(vmem_limit_bytes=16 << 20),
        cost_estimate=pl.CostEstimate(
            flops=2 * diffs.size * weight.shape[1], bytes_accessed=12 * diffs.size // 2,
            transcendentals=0,
        ),
    )(diffs, *grams, weight, base, keep)


def pair_kernel(own, other, out):
    out[0] = own[...]
    out[1] = other[...]


def classes_kernel(mine, up, down, two, two_far, out):
    out[0] = mine[...]
    out[1] = up[...]
    out[2] = down[...]
    out[3, :, 0] = two[...]
    out[3, :, 1] = two_far[...]


def pack(kernel, name, *parts):
    shape = ((2 if name == "pair" else 4),) + parts[0].shape
    return pl.pallas_call(
        kernel,
        out_shape=jax.ShapeDtypeStruct(shape, parts[0].dtype),
        in_specs=[vmem()] * len(parts),
        out_specs=vmem(),
        name=name,
        compiler_params=pltpu.CompilerParams(vmem_limit_bytes=4 << 20),
        cost_estimate=pl.CostEstimate(
            flops=0, bytes_accessed=4 * shape[0] * parts[0].size, transcendentals=0
        ),
    )(*parts)


def on_device(calib, base_weight, keep_blocks):
    tokens = calib.shape[0] * 8
    feats = calib.T
    own = lax.all_gather(feats, "zh", axis=0, tiled=True)
    other = lax.ppermute(own, "ylo", SWAP)
    near = lax.optimization_barrier((feats, own))[0]
    rows = [feats] + [lax.ppermute(near, "zl", [((i + d) % 4, i) for i in range(4)]) for d in (1, 2, 3)]
    other, *rows[1:] = lax.optimization_barrier((other, *rows[1:]))
    cols = pack(pair_kernel, "pair", own, other)
    mates = lax.ppermute(cols, "core", SWAP)

    base_weight = lax.optimization_barrier((base_weight, cols))[0]
    weight, diff, keep = start(keep_blocks, base_weight)
    diff, mates = lax.optimization_barrier((diff, mates))
    term = partial_gram(rows, cols, mates)
    terms = lax.all_to_all(term, ROW, 0, 0, tiled=True)
    gram = (jnp.sum(terms.astype(jnp.float32), axis=0) / tokens).astype(jnp.bfloat16)

    line = ("zh", "zl", "core")
    far_gram = lax.ppermute(gram, "ylo", SWAP)
    diff = lax.optimization_barrier((diff, far_gram))[0]
    diffs = lax.all_to_all(diff, ROW, 0, 0, tiled=True)
    mine = lax.all_gather(pack(pair_kernel, "pair", gram, far_gram), "zh", axis=0)
    diffs, mine = lax.optimization_barrier((diffs, mine))
    half = mine[:, 0]
    two = lax.ppermute(half, line, from_z(2, -2))
    up, down = (lax.ppermute(mine, line, from_z(s, s)) for s in (1, -1))
    two_far = lax.ppermute(two, "ylo", SWAP)
    packed = pack(classes_kernel, "classes", mine, up, down, two, two_far)
    grams = (packed, lax.ppermute(packed, "core", SWAP))

    weight, sent = step(False, diffs, grams, weight, base_weight, keep)
    diffs = lax.all_to_all(sent, ROW, 0, 0, tiled=True)
    return step(True, diffs, grams, weight, base_weight, keep)[0]


def solution(mesh):
    split = Mesh(mesh.devices.reshape(SIZES), AXES)
    return jax.shard_map(
        on_device,
        mesh=split,
        in_specs=(P(ROW, TOK), P(TOK, ROW), P()),
        out_specs=P(TOK, ROW),
        check_vma=False,
    )
```

```python
import functools

import jax
import jax.numpy as jnp
from jax import lax
from jax.experimental import pallas as pl
from jax.experimental.pallas import tpu as pltpu
from jax.sharding import Mesh, PartitionSpec as P

BLOCK = 128
RATE = 0.25
NT = (((1,), (1,)), ((), ()))
AXES = ("ylo", "zh", "zl", "core", "yhi", "x")
SIZES = (2, 4, 4, 2, 2, 4)
TOK = ("ylo", "zh", "zl", "core")
ROW = ("yhi", "x")
SWAP = ((0, 1), (1, 0))
CLASSES = (0, 1, 3, 2)


def from_z(*steps):
    return [((z + s) % 16 * 2 + c, z * 2 + c) for z in range(16) for c, s in enumerate(steps)]


def vmem():
    return pl.BlockSpec(memory_space=pltpu.VMEM)


def smem():
    return pl.BlockSpec(memory_space=pltpu.SMEM)


def by_core(x):
    chunk = BLOCK // 2
    order = [2 * i + c for c in range(2) for i in range(x.shape[1] // BLOCK)]
    return jnp.concatenate([x[:, i * chunk : (i + 1) * chunk] for i in order], axis=1)


def start_kernel(kept, base, weight, diff, keep_out):
    tok = lax.axis_index(TOK)
    first = lax.axis_index(ROW) * (base.shape[1] // BLOCK)
    block = lax.broadcasted_iota(jnp.int32, base.shape, 1) // BLOCK
    keep = jnp.zeros(base.shape, jnp.float32)
    for b in range(base.shape[1] // BLOCK):
        listed = jnp.int32(0)
        for j in range(kept.shape[0]):
            listed = jnp.where(kept[j, tok] == first + b, 1, listed)
        keep = jnp.where(block == b, listed.astype(jnp.float32), keep)
    base_float = base[...].astype(jnp.float32)
    new = (keep * base_float).astype(jnp.bfloat16)
    weight[...] = new
    keep_out[...] = keep
    sent = by_core((new.astype(jnp.float32) - base_float).astype(jnp.bfloat16))
    for i in range(diff.shape[0]):
        diff[i] = sent


def start(keep_blocks, base):
    bf16 = jax.ShapeDtypeStruct(base.shape, base.dtype)
    return pl.pallas_call(
        start_kernel,
        out_shape=(
            bf16,
            jax.ShapeDtypeStruct((8,) + base.shape, base.dtype),
            jax.ShapeDtypeStruct(base.shape, jnp.float32),
        ),
        in_specs=[smem(), vmem()],
        out_specs=(vmem(),) * 3,
        name="start",
        compiler_params=pltpu.CompilerParams(vmem_limit_bytes=4 << 20),
    )(keep_blocks.T, base)


def partial_gram_kernel(r0, r1, r2, r3, cols, mates, out, rows):
    ylo, zl, core = (lax.axis_index(a) for a in ("ylo", "zl", "core"))
    chunk = BLOCK // 2
    for d, part in enumerate((r0, r1, r2, r3)):
        place = lax.rem(zl + d, 4) * chunk
        rows[pl.ds(pl.multiple_of(place, chunk), chunk), :] = part[...]
    for dy, dc, part in ((0, 0, cols), (1, 0, cols), (0, 1, mates), (1, 1, mates)):
        term = lax.dot_general(part[dy], rows[...], NT, preferred_element_type=jnp.float32)
        term = term.astype(jnp.bfloat16).reshape(4, chunk, rows.shape[0])
        half = pl.ds(pl.multiple_of((core ^ dc) * chunk, chunk), chunk)
        out[pl.ds((ylo ^ dy) * 4, 4), half, :] = term


def partial_gram(rows, *cols):
    k, depth = cols[0].shape[1:]
    return pl.pallas_call(
        partial_gram_kernel,
        out_shape=jax.ShapeDtypeStruct((8, BLOCK, k), jnp.bfloat16),
        in_specs=[vmem()] * 6,
        out_specs=vmem(),
        scratch_shapes=[pltpu.VMEM((k, depth), jnp.bfloat16)],
        name="partial_gram",
        compiler_params=pltpu.CompilerParams(vmem_limit_bytes=8 << 20),
        cost_estimate=pl.CostEstimate(
            flops=8 * k * k * depth, bytes_accessed=12 * k * depth, transcendentals=0
        ),
    )(*rows, *cols)


def step_kernel(last, diffs, *refs):
    grams, (weight, base, keep), outs, total = refs[:2], refs[2:5], refs[5:-1], refs[-1]
    zl, core = lax.axis_index("zl"), lax.axis_index("core")
    half = grams[0].shape[4]
    for j, shift in enumerate(CLASSES):
        part = jnp.zeros((weight.shape[0], BLOCK), jnp.float32)
        for c in range(2):
            lanes = pl.ds(pl.multiple_of((core ^ c) * half, half), half)
            for h in range(4):
                for y in range(2):
                    part += lax.dot_general(
                        diffs[y * 4 + h, :, lanes], grams[c][j, h, y], NT,
                        preferred_element_type=jnp.float32,
                    )
        place = lax.rem(zl + shift, 4) * BLOCK
        total[:, pl.ds(pl.multiple_of(place, BLOCK), BLOCK)] = part
    old = weight[...].astype(jnp.float32)
    new = (old - RATE * keep[...] * total[...]).astype(jnp.bfloat16)
    outs[0][...] = new
    if not last:
        diff = (new.astype(jnp.float32) - base[...].astype(jnp.float32)).astype(jnp.bfloat16)
        diff = by_core(diff)
        for i in range(outs[1].shape[0]):
            outs[1][i] = diff


def step(last, diffs, grams, weight, base, keep):
    shape = jax.ShapeDtypeStruct(weight.shape, weight.dtype)
    outs = (shape,) if last else (shape, jax.ShapeDtypeStruct(diffs.shape, diffs.dtype))
    return pl.pallas_call(
        functools.partial(step_kernel, last),
        out_shape=outs,
        in_specs=[vmem()] * (len(grams) + 4),
        out_specs=tuple(vmem() for _ in outs),
        scratch_shapes=[pltpu.VMEM(weight.shape, jnp.float32)],
        name="last_step" if last else "first_step",
        compiler_params=pltpu.CompilerParams(vmem_limit_bytes=16 << 20),
        cost_estimate=pl.CostEstimate(
            flops=2 * diffs.size * weight.shape[1], bytes_accessed=12 * diffs.size // 2,
            transcendentals=0,
        ),
    )(diffs, *grams, weight, base, keep)


def pair_kernel(own, other, out):
    out[0] = own[...]
    out[1] = other[...]


def classes_kernel(mine, up, down, two, two_far, out):
    ylo = lax.axis_index("ylo")
    out[0] = mine[...]
    out[1] = up[...]
    out[2] = down[...]
    out[3, :, ylo] = two[...]
    out[3, :, 1 - ylo] = two_far[...]


def pack(kernel, name, *parts):
    shape = ((2 if name == "pair" else 4),) + parts[0].shape
    return pl.pallas_call(
        kernel,
        out_shape=jax.ShapeDtypeStruct(shape, parts[0].dtype),
        in_specs=[vmem()] * len(parts),
        out_specs=vmem(),
        name=name,
        compiler_params=pltpu.CompilerParams(vmem_limit_bytes=4 << 20),
        cost_estimate=pl.CostEstimate(
            flops=0, bytes_accessed=4 * shape[0] * parts[0].size, transcendentals=0
        ),
    )(*parts)


def on_device(calib, base_weight, keep_blocks):
    tokens = calib.shape[0] * 8
    feats = calib.T
    own = lax.all_gather(feats, "zh", axis=0, tiled=True)
    other = lax.ppermute(own, "ylo", SWAP)
    near = lax.optimization_barrier((feats, own))[0]
    parts = {d: lax.ppermute(near, "zl", [((i + d) % 4, i) for i in range(4)]) for d in (1, 3, 2)}
    rows = [feats, parts[1], parts[2], parts[3]]
    other, rows[1], rows[3], rows[2] = lax.optimization_barrier((other, rows[1], rows[3], rows[2]))
    cols = pack(pair_kernel, "pair", own, other)
    mates = lax.ppermute(cols, "core", SWAP)

    base_weight = lax.optimization_barrier((base_weight, cols))[0]
    weight, diff, keep = start(keep_blocks, base_weight)
    diff, mates = lax.optimization_barrier((diff, mates))
    term = partial_gram(rows, cols, mates)
    terms = lax.all_to_all(term, ROW, 0, 0, tiled=True)
    gram = (jnp.sum(terms.astype(jnp.float32), axis=0) / tokens).astype(jnp.bfloat16)

    line = ("zh", "zl", "core")
    gram = lax.all_gather(gram, "ylo", axis=0)
    diff = lax.optimization_barrier((diff, gram))[0]
    diffs = lax.all_to_all(diff, ROW, 0, 0, tiled=True)
    mine = lax.all_gather(gram, "zh", axis=0)
    diffs, mine = lax.optimization_barrier((diffs, mine))
    half = lax.dynamic_index_in_dim(mine, lax.axis_index("ylo"), 1, keepdims=False)
    two = lax.ppermute(half, line, from_z(2, -2))
    up, down = (lax.ppermute(mine, line, from_z(s, s)) for s in (1, -1))
    two_far = lax.ppermute(two, "ylo", SWAP)
    packed = pack(classes_kernel, "classes", mine, up, down, two, two_far)
    grams = (packed, lax.ppermute(packed, "core", SWAP))

    weight, sent = step(False, diffs, grams, weight, base_weight, keep)
    diffs = lax.all_to_all(sent, ROW, 0, 0, tiled=True)
    return step(True, diffs, grams, weight, base_weight, keep)[0]


def solution(mesh):
    split = Mesh(mesh.devices.reshape(SIZES), AXES)
    return jax.shard_map(
        on_device,
        mesh=split,
        in_specs=(P(ROW, TOK), P(TOK, ROW), P()),
        out_specs=P(TOK, ROW),
        check_vma=False,
    )
```

```python
import functools

import jax
import jax.numpy as jnp
from jax import lax
from jax.experimental import pallas as pl
from jax.experimental.pallas import tpu as pltpu
from jax.sharding import Mesh, PartitionSpec as P

BLOCK = 128
RATE = 0.25
NT = (((1,), (1,)), ((), ()))
AXES = ("ylo", "zh", "zl", "core", "yhi", "x")
SIZES = (2, 4, 4, 2, 2, 4)
TOK = ("ylo", "zh", "zl", "core")
ROW = ("yhi", "x")
SWAP = ((0, 1), (1, 0))
CLASSES = (0, 1, 3, 2)


def from_z(*steps):
    return [((z + s) % 16 * 2 + c, z * 2 + c) for z in range(16) for c, s in enumerate(steps)]


def vmem():
    return pl.BlockSpec(memory_space=pltpu.VMEM)


def smem():
    return pl.BlockSpec(memory_space=pltpu.SMEM)


def by_core(x):
    chunk = BLOCK // 2
    order = [2 * i + c for c in range(2) for i in range(x.shape[1] // BLOCK)]
    return jnp.concatenate([x[:, i * chunk : (i + 1) * chunk] for i in order], axis=1)


def start_kernel(kept, base, weight, diff, keep_out):
    tok = lax.axis_index(TOK)
    first = lax.axis_index(ROW) * (base.shape[1] // BLOCK)
    block = lax.broadcasted_iota(jnp.int32, base.shape, 1) // BLOCK
    keep = jnp.zeros(base.shape, jnp.float32)
    for b in range(base.shape[1] // BLOCK):
        listed = jnp.int32(0)
        for j in range(kept.shape[0]):
            listed = jnp.where(kept[j, tok] == first + b, 1, listed)
        keep = jnp.where(block == b, listed.astype(jnp.float32), keep)
    base_float = base[...].astype(jnp.float32)
    new = (keep * base_float).astype(jnp.bfloat16)
    weight[...] = new
    keep_out[...] = keep
    sent = by_core((new.astype(jnp.float32) - base_float).astype(jnp.bfloat16))
    for i in range(diff.shape[0]):
        diff[i] = sent


def start(keep_blocks, base):
    bf16 = jax.ShapeDtypeStruct(base.shape, base.dtype)
    return pl.pallas_call(
        start_kernel,
        out_shape=(
            bf16,
            jax.ShapeDtypeStruct((8,) + base.shape, base.dtype),
            jax.ShapeDtypeStruct(base.shape, jnp.float32),
        ),
        in_specs=[smem(), vmem()],
        out_specs=(vmem(),) * 3,
        name="start",
        compiler_params=pltpu.CompilerParams(vmem_limit_bytes=4 << 20),
    )(keep_blocks.T, base)


def partial_gram_kernel(r0, r1, r2, r3, cols, mates, out, rows):
    ylo, zl, core = (lax.axis_index(a) for a in ("ylo", "zl", "core"))
    chunk = BLOCK // 2
    for d, part in enumerate((r0, r1, r2, r3)):
        place = lax.rem(zl + d, 4) * chunk
        rows[pl.ds(pl.multiple_of(place, chunk), chunk), :] = part[...]
    for dy, dc, part in ((0, 0, cols), (1, 0, cols), (0, 1, mates), (1, 1, mates)):
        term = lax.dot_general(part[dy], rows[...], NT, preferred_element_type=jnp.float32)
        term = term.astype(jnp.bfloat16).reshape(4, chunk, rows.shape[0])
        half = pl.ds(pl.multiple_of((core ^ dc) * chunk, chunk), chunk)
        out[pl.ds((ylo ^ dy) * 4, 4), half, :] = term


def partial_gram(rows, *cols):
    k, depth = cols[0].shape[1:]
    return pl.pallas_call(
        partial_gram_kernel,
        out_shape=jax.ShapeDtypeStruct((8, BLOCK, k), jnp.bfloat16),
        in_specs=[vmem()] * 6,
        out_specs=vmem(),
        scratch_shapes=[pltpu.VMEM((k, depth), jnp.bfloat16)],
        name="partial_gram",
        compiler_params=pltpu.CompilerParams(vmem_limit_bytes=8 << 20),
        cost_estimate=pl.CostEstimate(
            flops=8 * k * k * depth, bytes_accessed=12 * k * depth, transcendentals=0
        ),
    )(*rows, *cols)


def step_kernel(last, diffs, *refs):
    grams, (weight, base, keep), outs, total = refs[:2], refs[2:5], refs[5:-1], refs[-1]
    zl, core = lax.axis_index("zl"), lax.axis_index("core")
    half = grams[0].shape[4]
    for j, shift in enumerate(CLASSES):
        part = jnp.zeros((weight.shape[0], BLOCK), jnp.float32)
        for c in range(2):
            lanes = pl.ds(pl.multiple_of((core ^ c) * half, half), half)
            for h in range(4):
                for y in range(2):
                    part += lax.dot_general(
                        diffs[y * 4 + h, :, lanes], grams[c][j, h, y], NT,
                        preferred_element_type=jnp.float32,
                    )
        place = lax.rem(zl + shift, 4) * BLOCK
        total[:, pl.ds(pl.multiple_of(place, BLOCK), BLOCK)] = part
    old = weight[...].astype(jnp.float32)
    new = (old - RATE * keep[...] * total[...]).astype(jnp.bfloat16)
    outs[0][...] = new
    if not last:
        diff = (new.astype(jnp.float32) - base[...].astype(jnp.float32)).astype(jnp.bfloat16)
        diff = by_core(diff)
        for i in range(outs[1].shape[0]):
            outs[1][i] = diff


def step(last, diffs, grams, weight, base, keep):
    shape = jax.ShapeDtypeStruct(weight.shape, weight.dtype)
    outs = (shape,) if last else (shape, jax.ShapeDtypeStruct(diffs.shape, diffs.dtype))
    return pl.pallas_call(
        functools.partial(step_kernel, last),
        out_shape=outs,
        in_specs=[vmem()] * (len(grams) + 4),
        out_specs=tuple(vmem() for _ in outs),
        scratch_shapes=[pltpu.VMEM(weight.shape, jnp.float32)],
        name="last_step" if last else "first_step",
        compiler_params=pltpu.CompilerParams(vmem_limit_bytes=16 << 20),
        cost_estimate=pl.CostEstimate(
            flops=2 * diffs.size * weight.shape[1], bytes_accessed=12 * diffs.size // 2,
            transcendentals=0,
        ),
    )(diffs, *grams, weight, base, keep)


def pair_kernel(own, other, out):
    out[0] = own[...]
    out[1] = other[...]


def classes_kernel(*refs):
    for i, ref in enumerate(refs[:-1]):
        refs[-1][i] = ref[...]


def pack(kernel, name, *parts):
    shape = ((2 if name == "pair" else 4),) + parts[0].shape
    return pl.pallas_call(
        kernel,
        out_shape=jax.ShapeDtypeStruct(shape, parts[0].dtype),
        in_specs=[vmem()] * len(parts),
        out_specs=vmem(),
        name=name,
        compiler_params=pltpu.CompilerParams(vmem_limit_bytes=4 << 20),
        cost_estimate=pl.CostEstimate(
            flops=0, bytes_accessed=4 * shape[0] * parts[0].size, transcendentals=0
        ),
    )(*parts)


def on_device(calib, base_weight, keep_blocks):
    tokens = calib.shape[0] * 8
    feats = calib.T
    own = lax.all_gather(feats, "zh", axis=0, tiled=True)
    other = lax.ppermute(own, "ylo", SWAP)
    near = lax.optimization_barrier((feats, own))[0]
    parts = {d: lax.ppermute(near, "zl", [((i + d) % 4, i) for i in range(4)]) for d in (1, 3, 2)}
    rows = [feats, parts[1], parts[2], parts[3]]
    other, rows[1], rows[3], rows[2] = lax.optimization_barrier((other, rows[1], rows[3], rows[2]))
    cols = pack(pair_kernel, "pair", own, other)
    mates = lax.ppermute(cols, "core", SWAP)

    base_weight = lax.optimization_barrier((base_weight, cols))[0]
    weight, diff, keep = start(keep_blocks, base_weight)
    diff, mates = lax.optimization_barrier((diff, mates))
    term = partial_gram(rows, cols, mates)
    terms = lax.all_to_all(term, ROW, 0, 0, tiled=True)
    gram = (jnp.sum(terms.astype(jnp.float32), axis=0) / tokens).astype(jnp.bfloat16)

    line = ("zh", "zl", "core")
    gram = lax.all_gather(gram, "ylo", axis=0)
    diff = lax.optimization_barrier((diff, gram))[0]
    diffs = lax.all_to_all(diff, ROW, 0, 0, tiled=True)
    mine = lax.all_gather(gram, "zh", axis=0)
    diffs, mine = lax.optimization_barrier((diffs, mine))
    two, up, down = (lax.ppermute(mine, line, from_z(*d)) for d in ((2, -2), (1, 1), (-1, -1)))
    packed = pack(classes_kernel, "classes", mine, up, down, two)
    grams = (packed, lax.ppermute(packed, "core", SWAP))

    weight, sent = step(False, diffs, grams, weight, base_weight, keep)
    diffs = lax.all_to_all(sent, ROW, 0, 0, tiled=True)
    return step(True, diffs, grams, weight, base_weight, keep)[0]


def solution(mesh):
    split = Mesh(mesh.devices.reshape(SIZES), AXES)
    return jax.shard_map(
        on_device,
        mesh=split,
        in_specs=(P(ROW, TOK), P(TOK, ROW), P()),
        out_specs=P(TOK, ROW),
        check_vma=False,
    )
```

```python
import functools

import jax
import jax.numpy as jnp
from jax import lax
from jax.experimental import pallas as pl
from jax.experimental.pallas import tpu as pltpu
from jax.sharding import Mesh, PartitionSpec as P

BLOCK = 128
RATE = 0.25
NT = (((1,), (1,)), ((), ()))
AXES = ("ylo", "zh", "zl", "core", "yhi", "x")
SIZES = (2, 4, 4, 2, 2, 4)
TOK = ("ylo", "zh", "zl", "core")
ROW = ("yhi", "x")
SWAP = ((0, 1), (1, 0))
CLASSES = (0, 1, 3, 2)


def from_z(*steps):
    return [((z + s) % 16 * 2 + c, z * 2 + c) for z in range(16) for c, s in enumerate(steps)]


def vmem():
    return pl.BlockSpec(memory_space=pltpu.VMEM)


def smem():
    return pl.BlockSpec(memory_space=pltpu.SMEM)


def by_core(x):
    chunk = BLOCK // 2
    order = [2 * i + c for c in range(2) for i in range(x.shape[1] // BLOCK)]
    return jnp.concatenate([x[:, i * chunk : (i + 1) * chunk] for i in order], axis=1)


def start_kernel(kept, base, weight, diff, keep_out):
    tok = lax.axis_index(TOK)
    first = lax.axis_index(ROW) * (base.shape[1] // BLOCK)
    block = lax.broadcasted_iota(jnp.int32, base.shape, 1) // BLOCK
    keep = jnp.zeros(base.shape, jnp.float32)
    for b in range(base.shape[1] // BLOCK):
        listed = jnp.int32(0)
        for j in range(kept.shape[0]):
            listed = jnp.where(kept[j, tok] == first + b, 1, listed)
        keep = jnp.where(block == b, listed.astype(jnp.float32), keep)
    base_float = base[...].astype(jnp.float32)
    new = (keep * base_float).astype(jnp.bfloat16)
    weight[...] = new
    keep_out[...] = keep
    sent = by_core((new.astype(jnp.float32) - base_float).astype(jnp.bfloat16))
    for i in range(diff.shape[0]):
        diff[i] = sent


def start(keep_blocks, base):
    bf16 = jax.ShapeDtypeStruct(base.shape, base.dtype)
    return pl.pallas_call(
        start_kernel,
        out_shape=(
            bf16,
            jax.ShapeDtypeStruct((8,) + base.shape, base.dtype),
            jax.ShapeDtypeStruct(base.shape, jnp.float32),
        ),
        in_specs=[smem(), vmem()],
        out_specs=(vmem(),) * 3,
        name="start",
        compiler_params=pltpu.CompilerParams(vmem_limit_bytes=4 << 20),
    )(keep_blocks.T, base)


def partial_gram_kernel(r0, r1, r2, r3, cols, mates, out, rows):
    ylo, zl, core = (lax.axis_index(a) for a in ("ylo", "zl", "core"))
    chunk = BLOCK // 2
    for d, part in enumerate((r0, r1, r2, r3)):
        place = lax.rem(zl + d, 4) * chunk
        rows[pl.ds(pl.multiple_of(place, chunk), chunk), :] = part[...]
    for dy, dc, part in ((0, 0, cols), (1, 0, cols), (0, 1, mates), (1, 1, mates)):
        term = lax.dot_general(part[dy], rows[...], NT, preferred_element_type=jnp.float32)
        term = term.astype(jnp.bfloat16).reshape(4, chunk, rows.shape[0])
        half = pl.ds(pl.multiple_of((core ^ dc) * chunk, chunk), chunk)
        out[pl.ds((ylo ^ dy) * 4, 4), half, :] = term


def partial_gram(rows, *cols):
    k, depth = cols[0].shape[1:]
    return pl.pallas_call(
        partial_gram_kernel,
        out_shape=jax.ShapeDtypeStruct((8, BLOCK, k), jnp.bfloat16),
        in_specs=[vmem()] * 6,
        out_specs=vmem(),
        scratch_shapes=[pltpu.VMEM((k, depth), jnp.bfloat16)],
        name="partial_gram",
        compiler_params=pltpu.CompilerParams(vmem_limit_bytes=8 << 20),
        cost_estimate=pl.CostEstimate(
            flops=8 * k * k * depth, bytes_accessed=12 * k * depth, transcendentals=0
        ),
    )(*rows, *cols)


def step_kernel(last, diffs, *refs):
    grams, (weight, base, keep), outs, total = refs[:2], refs[2:5], refs[5:-1], refs[-1]
    zl, core = lax.axis_index("zl"), lax.axis_index("core")
    half = grams[0].shape[4]
    for j, shift in enumerate(CLASSES):
        part = jnp.zeros((weight.shape[0], BLOCK), jnp.float32)
        for c in range(2):
            lanes = pl.ds(pl.multiple_of((core ^ c) * half, half), half)
            for h in range(4):
                for y in range(2):
                    part += lax.dot_general(
                        diffs[y * 4 + h, :, lanes], grams[c][j, h, y], NT,
                        preferred_element_type=jnp.float32,
                    )
        place = lax.rem(zl + shift, 4) * BLOCK
        total[:, pl.ds(pl.multiple_of(place, BLOCK), BLOCK)] = part
    old = weight[...].astype(jnp.float32)
    new = (old - RATE * keep[...] * total[...]).astype(jnp.bfloat16)
    outs[0][...] = new
    if not last:
        diff = (new.astype(jnp.float32) - base[...].astype(jnp.float32)).astype(jnp.bfloat16)
        diff = by_core(diff)
        for i in range(outs[1].shape[0]):
            outs[1][i] = diff


def step(last, diffs, grams, weight, base, keep):
    shape = jax.ShapeDtypeStruct(weight.shape, weight.dtype)
    outs = (shape,) if last else (shape, jax.ShapeDtypeStruct(diffs.shape, diffs.dtype))
    return pl.pallas_call(
        functools.partial(step_kernel, last),
        out_shape=outs,
        in_specs=[vmem()] * (len(grams) + 4),
        out_specs=tuple(vmem() for _ in outs),
        scratch_shapes=[pltpu.VMEM(weight.shape, jnp.float32)],
        name="last_step" if last else "first_step",
        compiler_params=pltpu.CompilerParams(vmem_limit_bytes=16 << 20),
        cost_estimate=pl.CostEstimate(
            flops=2 * diffs.size * weight.shape[1], bytes_accessed=12 * diffs.size // 2,
            transcendentals=0,
        ),
    )(diffs, *grams, weight, base, keep)


def pair_kernel(own, other, out):
    out[0] = own[...]
    out[1] = other[...]


def classes_kernel(mine, up, down, two, out):
    out[0] = mine[...]
    out[1] = up[...]
    out[2] = down[...]
    for y in range(2):
        out[3, :, y] = two[y]


def pack(kernel, name, *parts):
    shape = ((2 if name == "pair" else 4),) + parts[0].shape
    return pl.pallas_call(
        kernel,
        out_shape=jax.ShapeDtypeStruct(shape, parts[0].dtype),
        in_specs=[vmem()] * len(parts),
        out_specs=vmem(),
        name=name,
        compiler_params=pltpu.CompilerParams(vmem_limit_bytes=4 << 20),
        cost_estimate=pl.CostEstimate(
            flops=0, bytes_accessed=4 * shape[0] * parts[0].size, transcendentals=0
        ),
    )(*parts)


def on_device(calib, base_weight, keep_blocks):
    tokens = calib.shape[0] * 8
    feats = calib.T
    own = lax.all_gather(feats, "zh", axis=0, tiled=True)
    other = lax.ppermute(own, "ylo", SWAP)
    near = lax.optimization_barrier((feats, own))[0]
    parts = {d: lax.ppermute(near, "zl", [((i + d) % 4, i) for i in range(4)]) for d in (1, 3, 2)}
    rows = [feats, parts[1], parts[2], parts[3]]
    other, rows[1], rows[3], rows[2] = lax.optimization_barrier((other, rows[1], rows[3], rows[2]))
    cols = pack(pair_kernel, "pair", own, other)
    mates = lax.ppermute(cols, "core", SWAP)

    base_weight = lax.optimization_barrier((base_weight, cols))[0]
    weight, diff, keep = start(keep_blocks, base_weight)
    diff, mates = lax.optimization_barrier((diff, mates))
    term = partial_gram(rows, cols, mates)
    terms = lax.all_to_all(term, ROW, 0, 0, tiled=True)
    gram = (jnp.sum(terms.astype(jnp.float32), axis=0) / tokens).astype(jnp.bfloat16)

    line = ("zh", "zl", "core")
    gram = lax.all_gather(gram, "ylo", axis=0)
    diff = lax.optimization_barrier((diff, gram))[0]
    diffs = lax.all_to_all(diff, ROW, 0, 0, tiled=True)
    mine = lax.all_gather(gram, "zh", axis=0)
    diffs, mine = lax.optimization_barrier((diffs, mine))
    half = lax.dynamic_index_in_dim(mine, lax.axis_index("ylo"), 1, keepdims=False)
    two = lax.ppermute(half, line, from_z(2, -2))
    up, down = (lax.ppermute(mine, line, from_z(s, s)) for s in (1, -1))
    packed = pack(classes_kernel, "classes", mine, up, down, lax.all_gather(two, "ylo", axis=0))
    grams = (packed, lax.ppermute(packed, "core", SWAP))

    weight, sent = step(False, diffs, grams, weight, base_weight, keep)
    diffs = lax.all_to_all(sent, ROW, 0, 0, tiled=True)
    return step(True, diffs, grams, weight, base_weight, keep)[0]


def solution(mesh):
    split = Mesh(mesh.devices.reshape(SIZES), AXES)
    return jax.shard_map(
        on_device,
        mesh=split,
        in_specs=(P(ROW, TOK), P(TOK, ROW), P()),
        out_specs=P(TOK, ROW),
        check_vma=False,
    )
```
